512 devices in a mesh: grp: 32 (over y, x, core), sub: 16 (over z).
Axes of the slice: x: 4, y: 4, z: 16, core: 2. Of those that a mesh axis runs over, the one named last changes fastest.
Arguments:
- loads: bfloat16 [32, 16, 16, 1536], P('grp', 'sub'), may hold values from -6 to 6
- boundary_values: float32 [16, 6144], replicated, may hold values from -6 to 6
- dirichlet_ids: int32 [32, 16, 3, 128], P('grp', 'sub'), may hold values from 0 to 6143
- dirichlet_coupling: bfloat16 [32, 16, 3, 512, 128], P('grp', 'sub'), may hold values from -0.5 to 0.5
- local_inverse: bfloat16 [32, 16, 3, 512, 512], P('grp', 'sub'), as said below
- local_schur: bfloat16 [32, 16, 3, 512, 512], P('grp', 'sub')
- corner_coupling: bfloat16 [32, 16, 3, 24, 512], P('grp', 'sub'), may hold values from -0.25 to 0.25
- corner_ids: int32 [32, 16, 3, 24], P('grp', 'sub'), may hold values from 0 to 12287
- coarse_inverse: bfloat16 [12288, 12288], P(('grp', 'sub')), as said below
- row_counts: int32 [32, 16, 18], P('grp', 'sub'), may hold values from 0 to 256, as said below
- slot_of: int32 [32, 16, 1536], P('grp', 'sub'), may hold values from 0 to 1535, each once within a row
Outputs:
- multipliers: float32 [32, 16, 16, 1536], P('grp', 'sub')
- residual: float32 [32, 16, 16, 1536], P('grp', 'sub')
The draws below stay inside these ranges and needn't reach their ends.
Inputs may be any that keep to these rules, and one draw needn't show every extreme that they name: row_counts[g, s, p] for p < 16 equals row_counts[g, p, s], is 0 for p = s and lies in 1 to 64 otherwise; every device reaches 64 with some peer. Column 16 of device (g, s) equals column 17 of device (g - 1, s), lies in 1 to 256, reaches 256 on some device of every slab boundary, and is 0 in the first slab; column 17 is 0 in the last slab. coarse_inverse is symmetric and positive definite. local_inverse and local_schur are symmetric and positive definite.
All inputs are finite; a program needn't handle non-finite values.
Results may differ from the reference program's by a relative error of at most 0.012.
Values may be sent and summed in bfloat16 or wider, within the bound.
No kernel may reach another device: no remote copies, remote signals or barrier semaphores. Data moves between devices by JAX's collectives and lax.ppermute only.
A program may use at most 64 MiB of HBM per device.

```python
import math
import jax
import jax.numpy as jnp
from jax import lax

IFACE = 512
SUBS_DEV = 3
LOADS = 16
CORNERS = 24
FIXED_DOFS = 128
BOUNDARY = 6144
SLAB_ROWS = 256
ITERS = 2
SLOTS = 1536
PEER_ROWS = 64
COARSE = 12288
N_GRP = 32
N_SUB = 16


def symmetric_block(key, lead, order, scale):
    first, second = jax.random.split(key)
    shape = lead + (order, order)
    base = jax.random.normal(first, shape, jnp.float32)
    mixed = (base + jnp.swapaxes(base, -1, -2)) * (scale / math.sqrt(2.0 * order))
    diagonal = jnp.exp(jax.random.uniform(second, lead + (order, 1), jnp.float32, 0.0, math.log(4.0)))
    identity = jnp.eye(order, dtype=jnp.float32)
    return mixed * (1.0 - identity) + identity * diagonal


def draw_local_inverse(key, part):
    return symmetric_block(jax.random.fold_in(key, 11), (N_GRP, N_SUB, SUBS_DEV), IFACE, 0.45).astype(jnp.bfloat16)


def draw_local_schur(key, part):
    return symmetric_block(jax.random.fold_in(key, 23), (N_GRP, N_SUB, SUBS_DEV), IFACE, 0.45).astype(jnp.bfloat16)


def draw_coarse_inverse(key, part):
    return symmetric_block(jax.random.fold_in(key, 37), (), COARSE, 0.45).astype(jnp.bfloat16)


def draw_row_counts(key, part):
    first, second = jax.random.split(jax.random.fold_in(key, 41))
    paired = jax.random.randint(first, (N_GRP, N_SUB, N_SUB), max(1, PEER_ROWS // 3), PEER_ROWS + 1)
    index = jnp.arange(N_SUB, dtype=jnp.int32)
    upper_half = (index[:, None] < index[None, :])[None]
    mirror = jnp.where(upper_half, paired, jnp.swapaxes(paired, 1, 2))
    mates = (index[:, None] ^ 1 == index[None, :])[None]
    mirror = jnp.where(mates, PEER_ROWS, mirror)
    mirror = jnp.where((index[:, None] == index[None, :])[None], 0, mirror)
    slab = jax.random.randint(second, (N_GRP, N_SUB), max(1, SLAB_ROWS // 3), SLAB_ROWS + 1)
    slab = jnp.where(index[None, :] == 0, SLAB_ROWS, slab)
    groups = jnp.arange(N_GRP, dtype=jnp.int32)[:, None]
    above = jnp.where(groups < N_GRP - 1, slab, 0)
    below = jnp.concatenate([jnp.zeros((1, N_SUB), jnp.int32), above[:-1]], axis=0)
    return jnp.concatenate([mirror, below[:, :, None], above[:, :, None]], axis=2).astype(jnp.int32)


def plant(values, own_key, low, high):
    spot = [jax.random.randint(jax.random.fold_in(own_key, axis), (), 0, length) for axis, length in enumerate(values.shape)]
    longest = values.shape.index(max(values.shape))
    beside = spot[:longest] + [(spot[longest] + 1) % values.shape[longest]] + spot[longest + 1:]
    return values.at[tuple(spot)].set(low).at[tuple(beside)].set(high)


def block_levels(key, shape, pieces, least, high):
    loudness = 1.0
    for dim, blocks in pieces:
        steps = jax.random.uniform(jax.random.fold_in(jax.random.fold_in(key, 6), dim), (blocks,), jnp.float32, least / len(pieces), high / len(pieces))
        loudness = loudness * jnp.repeat(jnp.exp(steps), shape[dim] // blocks).reshape((-1,) + (1,) * (len(shape) - 1 - dim))
    return loudness


def gaussian(own_key, shape, width, limit, cuts=(), held_as=jnp.bfloat16):
    entries = width * jax.random.normal(own_key, shape, jnp.float32)
    if cuts:
        entries = entries * block_levels(own_key, shape, cuts, -0.22, 0.18)
    return jnp.clip(entries, -limit, limit).astype(held_as)


def setup_inputs(seed: int = 0) -> dict:
    arg_keys = jax.random.split(jax.random.key(seed), 12)
    loads = gaussian(arg_keys[0], (N_GRP, N_SUB, LOADS, SLOTS), 1.0, 6.0, ((0, 32), (1, 16)))
    boundary_values = gaussian(arg_keys[1], (LOADS, BOUNDARY), 1.0, 6.0, (), jnp.float32)
    dirichlet_ids = plant(jax.random.randint(arg_keys[2], (N_GRP, N_SUB, SUBS_DEV, FIXED_DOFS), 0, BOUNDARY), jax.random.fold_in(arg_keys[2], 1), 0, BOUNDARY - 1).astype(jnp.int32)
    dirichlet_coupling = gaussian(arg_keys[3], (N_GRP, N_SUB, SUBS_DEV, IFACE, FIXED_DOFS), FIXED_DOFS ** -0.5, 0.5, ((0, 32), (1, 16)))
    local_inverse = draw_local_inverse(jax.random.fold_in(arg_keys[11], 71), 0)
    local_schur = draw_local_schur(jax.random.fold_in(arg_keys[11], 71), 0)
    corner_coupling = gaussian(arg_keys[6], (N_GRP, N_SUB, SUBS_DEV, CORNERS, IFACE), IFACE ** -0.5, 0.25, ((0, 32), (1, 16)))
    corner_ids = plant(jax.random.randint(arg_keys[7], (N_GRP, N_SUB, SUBS_DEV, CORNERS), 0, COARSE), jax.random.fold_in(arg_keys[7], 1), 0, COARSE - 1).astype(jnp.int32)
    coarse_inverse = draw_coarse_inverse(jax.random.fold_in(arg_keys[11], 71), 0)
    row_counts = draw_row_counts(jax.random.fold_in(arg_keys[11], 71), 0)
    slot_of = jax.vmap(lambda own: jax.random.permutation(own, SLOTS))(jax.random.split(arg_keys[10], N_GRP * N_SUB)).reshape((N_GRP, N_SUB, SLOTS)).astype(jnp.int32)
    return {"loads": loads, "boundary_values": boundary_values, "dirichlet_ids": dirichlet_ids, "dirichlet_coupling": dirichlet_coupling, "local_inverse": local_inverse, "local_schur": local_schur, "corner_coupling": corner_coupling, "corner_ids": corner_ids, "coarse_inverse": coarse_inverse, "row_counts": row_counts, "slot_of": slot_of}


def slot_tables(row_counts, slot_of):
    length = SUBS_DEV * IFACE
    within = N_SUB * PEER_ROWS
    positions = jnp.arange(length, dtype=jnp.int32)
    inverse = jax.vmap(jax.vmap(lambda order: jnp.zeros(length, jnp.int32).at[order].set(positions)))(slot_of)
    column = jnp.where(positions < within, positions // PEER_ROWS, N_SUB + (positions - within) // SLAB_ROWS).astype(jnp.int32)
    offset = jnp.where(positions < within, positions % PEER_ROWS, (positions - within) % SLAB_ROWS).astype(jnp.int32)
    counts = jnp.take(row_counts, column, axis=2)
    canon_live = (offset[None, None, :] < counts).astype(jnp.float32)
    live = jnp.take_along_axis(canon_live, inverse, axis=2)
    return inverse, live


def partner(values, slot_of, inverse):
    within = N_SUB * PEER_ROWS
    canon = jnp.take_along_axis(values, jnp.broadcast_to(slot_of[:, :, None, :], values.shape), axis=3)
    inner_part = canon[..., :within].reshape(N_GRP, N_SUB, LOADS, N_SUB, PEER_ROWS)
    paired = jnp.transpose(inner_part, (0, 3, 2, 1, 4)).reshape(N_GRP, N_SUB, LOADS, within)
    lower_side = canon[..., within:within + SLAB_ROWS]
    upper_side = canon[..., within + SLAB_ROWS:]
    from_below = jnp.concatenate([jnp.zeros_like(upper_side[:1]), upper_side[:-1]], axis=0)
    from_above = jnp.concatenate([lower_side[1:], jnp.zeros_like(lower_side[:1])], axis=0)
    joined = jnp.concatenate([paired, from_below, from_above], axis=3)
    return jnp.take_along_axis(joined, jnp.broadcast_to(inverse[:, :, None, :], values.shape), axis=3)


def block_apply(matrices, field_b):
    blocks = field_b.reshape(N_GRP * N_SUB, LOADS, SUBS_DEV, IFACE)

    def one_device(pair):
        matrix, vector = pair
        return jnp.einsum('anm,ram->ran', matrix.astype(jnp.float32), vector.astype(jnp.float32))

    result = lax.map(one_device, (matrices.reshape(N_GRP * N_SUB, SUBS_DEV, IFACE, IFACE), blocks))
    return result.reshape(N_GRP, N_SUB, LOADS, SUBS_DEV * IFACE)


def apply_tilde(field_b, local_inverse, corner_coupling, corner_ids, coarse_inverse):
    local_part = block_apply(local_inverse, field_b)
    blocks = field_b.reshape(N_GRP, N_SUB, LOADS, SUBS_DEV, IFACE).astype(jnp.float32)
    coupling = corner_coupling.astype(jnp.float32)
    corner_terms = jnp.einsum('gsacm,gsram->rgsac', coupling, blocks).reshape(LOADS, -1)
    flat_ids = corner_ids.reshape(-1)
    coarse_load = jnp.zeros((LOADS, COARSE), jnp.float32).at[:, flat_ids].add(corner_terms)
    coarse_values = jnp.dot(coarse_load.astype(jnp.bfloat16), coarse_inverse.T, preferred_element_type=jnp.float32)
    at_corners = coarse_values[:, flat_ids].astype(jnp.bfloat16).astype(jnp.float32)
    at_corners = at_corners.reshape(LOADS, N_GRP, N_SUB, SUBS_DEV, CORNERS)
    correction = jnp.einsum('gsacm,rgsac->gsram', coupling, at_corners).reshape(N_GRP, N_SUB, LOADS, SUBS_DEV * IFACE)
    return local_part + correction


def reference(loads, boundary_values, dirichlet_ids, dirichlet_coupling, local_inverse, local_schur, corner_coupling, corner_ids, coarse_inverse, row_counts, slot_of):
    inverse, live = slot_tables(row_counts, slot_of)
    live_field = live[:, :, None, :]

    def jumps(values):
        return live_field * (values - partner(values, slot_of, inverse))

    def dual(field):
        return jumps(apply_tilde(field.astype(jnp.bfloat16), local_inverse, corner_coupling, corner_ids, coarse_inverse))

    picked = boundary_values[:, dirichlet_ids].astype(jnp.bfloat16).astype(jnp.float32)
    lifted_part = jnp.einsum('gsand,rgsad->gsran', dirichlet_coupling.astype(jnp.float32), picked)
    lifted_part = lifted_part.reshape(N_GRP, N_SUB, LOADS, SUBS_DEV * IFACE)
    lifted = live_field * (loads.astype(jnp.float32) - lifted_part)
    jump_field = dual(lifted)
    multipliers = jnp.zeros_like(jump_field)
    residual = jump_field
    search = jump_field
    inner_before = jnp.ones((LOADS,), jnp.float32)
    for step in range(ITERS):
        smoothed = block_apply(local_schur, residual.astype(jnp.bfloat16))
        precond = 0.25 * live_field * (smoothed - partner(smoothed, slot_of, inverse))
        inner_now = jnp.sum(residual * precond, axis=(0, 1, 3))
        if step == 0:
            search = precond
        else:
            search = precond + (inner_now / inner_before)[None, None, :, None] * search
        image = dual(search)
        curvature = jnp.sum(search * image, axis=(0, 1, 3))
        step_size = (inner_now / curvature)[None, None, :, None]
        multipliers = multipliers + step_size * search
        residual = residual - step_size * image
        inner_before = inner_now
    return multipliers, residual
```

```python
import jax
import jax.numpy as jnp
from jax import lax
from jax.experimental import pallas as pl
from jax.experimental.pallas import tpu as pltpu
from jax.sharding import PartitionSpec as P


IFACE = 512
SUBS = 3
LOADS = 16
CORNERS = 24
FIXED = 128
SLAB = 256
PEER = 64
N_GRP = 32
N_SUB = 16
LENGTH = SUBS * IFACE
WITHIN = N_SUB * PEER
LANES = 128
COARSE = 12288
ROWS = COARSE // N_GRP
COLS = COARSE // N_SUB
OWN = SUBS * CORNERS
BOUNDARY = 6144
F32 = jnp.float32
BF16 = jnp.bfloat16
VMEM_LIMIT = 48 * 1024 * 1024
OH_PARTS = 8
PICK_PARTS = 4
FIELD_PARTS = 6


def nt(a, b):
    return lax.dot_general(a, b, (((1,), (1,)), ((), ())), preferred_element_type=F32)


def nn(a, b):
    return jnp.dot(a, b, preferred_element_type=F32)


def iota(shape, dim):
    return lax.broadcasted_iota(jnp.int32, shape, dim)


def onehot(test):
    return jnp.where(test, 1.0, 0.0).astype(BF16)


def roll(x, shift):
    return pltpu.roll(x, shift, 1)


def call(body, outs, *args, smem=(), hbm=(), out_hbm=(), scratch=()):
    def place(i, chosen):
        if i in chosen:
            return pl.BlockSpec(memory_space=pltpu.HBM)
        return pl.BlockSpec(memory_space=pltpu.VMEM)

    specs = [
        pl.BlockSpec(memory_space=pltpu.SMEM) if i in smem else place(i, hbm) for i in range(len(args))
    ]
    args = [
        pltpu.with_memory_space_constraint(x, pltpu.HBM) if i in hbm else x for i, x in enumerate(args)
    ]
    return pl.pallas_call(
        body,
        out_shape=[
            pltpu.HBM(s, d) if i in out_hbm else jax.ShapeDtypeStruct(s, d)
            for i, (s, d) in enumerate(outs)
        ],
        in_specs=specs,
        out_specs=[place(i, out_hbm) for i in range(len(outs))],
        scratch_shapes=list(scratch),
        compiler_params=pltpu.CompilerParams(vmem_limit_bytes=VMEM_LIMIT),
    )(*args)


def started(pairs, sems):
    copies = [pltpu.make_async_copy(src, dst, sems.at[i]) for i, (src, dst) in enumerate(pairs)]
    for copy in copies:
        copy.start()
    return copies


def live_mask(counts):
    lane = iota((LOADS, LANES), 1)
    parts = []
    for k in range(N_SUB // 2):
        limit = jnp.where(lane < PEER, counts[0, 2 * k], counts[0, 2 * k + 1] + PEER)
        parts.append(lane < limit)
    for side in range(2):
        for half in range(2):
            parts.append(lane + LANES * half < counts[0, N_SUB + side])
    return [jnp.where(p, 1.0, 0.0) for p in parts]


def pack(y, peers, below, above):
    low = iota((8, LANES), 1) < PEER
    for k in range(N_SUB // 2):
        block = y[:, LANES * k : LANES * (k + 1)]
        top, bottom = block[:8], block[8:]
        peers[2 * k] = jnp.where(low, top, roll(bottom, PEER))
        peers[2 * k + 1] = jnp.where(low, roll(top, PEER), bottom)
    below[...] = y[:, WITHIN : WITHIN + SLAB]
    above[...] = y[:, WITHIN + SLAB :]


def unpack(peers, from_below, from_above):
    low = iota((8, LANES), 1) < PEER
    parts = []
    for k in range(N_SUB // 2):
        m, n = peers[2 * k], peers[2 * k + 1]
        top = jnp.where(low, m, roll(n, PEER))
        bottom = jnp.where(low, roll(m, PEER), n)
        parts.append(jnp.concatenate([top, bottom], axis=0))
    for ref in (from_below, from_above):
        parts += [ref[:, :LANES], ref[:, LANES:]]
    return parts


def jump(y, peers, from_below, from_above, counts, scale):
    masks = live_mask(counts)
    other = unpack(peers, from_below, from_above)
    parts = []
    for k in range(LENGTH // LANES):
        own = y[:, LANES * k : LANES * (k + 1)]
        parts.append(scale * masks[k] * (own - other[k]))
    return jnp.concatenate(parts, axis=1)


def split3(x):
    hi = x.astype(BF16)
    rest = x - hi.astype(F32)
    mid = rest.astype(BF16)
    low = (rest - mid.astype(F32)).astype(BF16)
    return hi, mid, low


def spread(x):
    hi, mid, low = (part.astype(F32) for part in split3(x))
    return hi + roll(mid, 8) + roll(low, 16)


def gathered(x):
    return x + roll(x, LANES - 8) + roll(x, LANES - 16)


def dot_rows(a, b):
    return jnp.sum(a * b, axis=1, keepdims=True)


def k_setup(
    bv_hbm, dids_hbm, dc_hbm, loads_hbm, slots_hbm, corner_hbm, ids, counts,
    u_out, chat_out, x_out, msg,
    bv, dids, dc, loads, slots, corner, u_buf, sems, out_sems,
):
    step = 768
    sources = (slots_hbm, dids_hbm, bv_hbm, corner_hbm, dc_hbm, loads_hbm)
    waits = started(tuple(zip(sources, (slots, dids, bv, corner, dc, loads))), sems)
    waits[0].wait()
    moves = []
    for a in range(SUBS):
        rows = slice(IFACE * a, IFACE * (a + 1))
        u_buf[rows, :] = onehot(iota((IFACE, LENGTH), 0) + IFACE * a == slots[...])
        moves.append(pltpu.make_async_copy(u_buf.at[rows, :], u_out.at[rows, :], out_sems.at[a]))
        moves[-1].start()
    for wait in waits[1:]:
        wait.wait()
    picked = jnp.zeros((LOADS, SUBS * FIXED), F32)
    for i in range(BOUNDARY // step):
        oh = onehot(iota((step, SUBS * FIXED), 0) + step * i == dids[...])
        picked += nn(bv[:, step * i : step * (i + 1)].astype(BF16), oh)
    picked = picked.astype(BF16)
    x = jnp.zeros((LOADS, LENGTH), F32)
    chat = []
    for a in range(SUBS):
        lifted = nt(picked[:, FIXED * a : FIXED * (a + 1)], dc[a])
        raw = (loads[:, IFACE * a : IFACE * (a + 1)].astype(F32) - lifted).astype(BF16)
        u = u_buf[IFACE * a : IFACE * (a + 1), :]
        x += nn(raw, u)
        chat.append(nn(corner[a], u))
    masks = live_mask(counts)
    x = jnp.concatenate(
        [masks[k] * x[:, LANES * k : LANES * (k + 1)] for k in range(LENGTH // LANES)], axis=1
    ).astype(BF16)
    x_out[...] = x
    chat.append(jnp.zeros((LANES - OWN, LENGTH), F32))
    chat = jnp.concatenate(chat, axis=0).astype(BF16)
    chat_out[...] = chat
    terms = nt(x, chat)
    row = iota((8, LANES), 0)
    high = jnp.broadcast_to(lax.shift_right_arithmetic(ids[...], 7), (8, LANES)).astype(F32)
    low = jnp.broadcast_to(jnp.bitwise_and(ids[...], 127), (8, LANES)).astype(F32)
    table = jnp.where(row == 0, high, jnp.where(row == 1, low, 0.0))
    tile = jnp.concatenate([terms, table], axis=0).astype(BF16)
    for g in range(N_GRP):
        msg[g] = tile
    for move in moves:
        move.wait()


def id_row(tile):
    tile = tile.astype(F32)
    return (tile[0:1] * 128.0 + tile[1:2]).astype(jnp.int32)


def k_load_first(recv, ids, where, oh_out, msg, oh_buf, sems):
    moves = []
    base = where[0, 0] * ROWS
    load = jnp.zeros((LOADS, ROWS), F32)
    for j in range(N_GRP // 2):
        pair = [recv[2 * j + i] for i in range(2)]
        row = jnp.concatenate([id_row(t[LOADS:]) for t in pair], axis=1)
        oh = onehot(iota((ROWS, 2 * LANES), 0) + base == row)
        oh_buf[j // 2, :, 2 * LANES * (j % 2) : 2 * LANES * (j % 2 + 1)] = oh
        if j % 2:
            moves.append(pltpu.make_async_copy(oh_buf.at[j // 2], oh_out.at[j // 2], sems.at[j // 2]))
            moves[-1].start()
        load += nt(jnp.concatenate([t[:LOADS] for t in pair], axis=1), oh)
    row = iota((8, LANES), 0)
    high = jnp.broadcast_to(lax.shift_right_arithmetic(ids[...], 7), (8, LANES)).astype(F32)
    low = jnp.broadcast_to(jnp.bitwise_and(ids[...], 127), (8, LANES)).astype(F32)
    table = jnp.where(row == 0, high, jnp.where(row == 1, low, 0.0))
    table = jnp.concatenate([table, jnp.zeros((8, ROWS - LANES), F32)], axis=1)
    tile = jnp.concatenate([load, table], axis=0).astype(BF16)
    for p in range(N_SUB):
        msg[p] = tile
    for move in moves:
        move.wait()


def k_load(recv, oh_hbm, msg, oh, sems):
    waits = started([(oh_hbm.at[i], oh.at[i]) for i in range(OH_PARTS)], sems)
    load = jnp.zeros((LOADS, ROWS), F32)
    for i, wait in enumerate(waits):
        terms = jnp.concatenate([recv[4 * i + g] for g in range(4)], axis=1)
        wait.wait()
        load += nt(terms, oh[i])
    load = load.astype(BF16)
    for p in range(N_SUB):
        msg[p] = load


def k_pick_table(recv, where, oh_out, oh_buf, sems):
    moves = []
    base = where[0, 1] * CORNERS
    dof = jnp.concatenate(
        [iota((CORNERS, LANES), 0) + (base + ROWS * g) for g in range(N_GRP)], axis=0
    )
    for p in range(N_SUB):
        row = id_row(recv[p, LOADS : LOADS + 8, :LANES])
        oh_buf[p // 4, :, LANES * (p % 4) : LANES * (p % 4 + 1)] = onehot(dof == row)
        if p % 4 == 3:
            moves.append(pltpu.make_async_copy(oh_buf.at[p // 4], oh_out.at[p // 4], sems.at[p // 4]))
            moves[-1].start()
    for move in moves:
        move.wait()


def slab_load(recv):
    total = recv[0, :LOADS, :].astype(F32)
    for p in range(1, N_SUB):
        total += recv[p, :LOADS, :].astype(F32)
    return total


def halves(x):
    hi = x.astype(BF16)
    return jnp.concatenate([hi, (x - hi.astype(F32)).astype(BF16)], axis=0)


def joined(x):
    if x.shape[0] == LOADS:
        return x[...]
    return x[:LOADS] + x[LOADS:]


def k_solve(recv, block, msg):
    values = joined(nt(halves(slab_load(recv)), block[...])).astype(BF16)
    for g in range(N_GRP):
        msg[g] = values


def k_solve_last(recv, block, gram, field, local, where, msg):
    load = slab_load(recv)
    values = joined(nt(halves(load), block[...])).astype(BF16)
    energy = dot_rows(field[...], joined(local))
    lane = iota((LOADS, LANES), 1)
    sums = roll(spread(jnp.where(lane == 4, energy, gram[...])), CORNERS)
    chunk = jnp.zeros((LOADS, LANES), F32)
    for s in range(N_SUB):
        piece = load[:, CORNERS * s : CORNERS * (s + 1)]
        piece = jnp.concatenate([piece, jnp.zeros((LOADS, LANES - CORNERS), F32)], axis=1)
        chunk = jnp.where(where[0, 1] == s, piece, chunk)
    sums = jnp.where(lane < CORNERS, chunk, sums)
    tile = jnp.concatenate([values, sums.astype(BF16)], axis=1)
    for g in range(N_GRP):
        msg[g] = tile


def coarse_sum(recv, start, size):
    total = recv[0, :, start : start + size].astype(F32)
    for g in range(1, N_GRP):
        total += recv[g, :, start : start + size].astype(F32)
    return total


def pick_starts(oh_hbm, oh, sems):
    return started([(oh_hbm.at[i], oh.at[i]) for i in range(PICK_PARTS)], sems)


def k_pick(recv, oh_hbm, msg, oh, sems):
    waits = pick_starts(oh_hbm, oh, sems)
    values = coarse_sum(recv, 0, COLS).astype(BF16)
    for i, wait in enumerate(waits):
        wait.wait()
        picked = nn(values, oh[i]).astype(BF16)
        for p in range(4):
            msg[4 * i + p] = picked[:, LANES * p : LANES * (p + 1)]


def k_pick_last(recv, oh_hbm, msg, oh, sems):
    waits = pick_starts(oh_hbm, oh, sems)
    values = coarse_sum(recv, 0, COLS)
    lane = iota((LOADS, LANES), 1)
    sums = jnp.where(lane < CORNERS, 0.0, coarse_sum(recv, COLS, LANES))
    sums = gathered(roll(sums, LANES - CORNERS))
    load = [recv[g, :, COLS : COLS + CORNERS].astype(F32) for g in range(N_GRP)]
    energy = dot_rows(jnp.concatenate(load, axis=1), values)
    sums = jnp.where(lane == 5, energy, jnp.where(lane < 5, sums, 0.0))
    sums = roll(spread(sums), OWN)
    values = values.astype(BF16)
    for i, wait in enumerate(waits):
        wait.wait()
        picked = nn(values, oh[i])
        for p in range(4):
            msg[4 * i + p] = (picked[:, LANES * p : LANES * (p + 1)] + sums).astype(BF16)


def corner_sum(recv):
    total = recv[0].astype(F32)
    for p in range(1, N_SUB):
        total += recv[p].astype(F32)
    return total


def k_correct(recv, chat, local, y_out, peers, below, above):
    y = joined(local) + nn(corner_sum(recv).astype(BF16), chat[...])
    y_out[...] = y
    pack(y, peers, below, above)


def k_correct_last(recv, chat, local, y_out, peers, below, above, sums_out):
    total = corner_sum(recv)
    lane = iota((LOADS, LANES), 1)
    at_corners = jnp.where(lane < OWN, total, 0.0).astype(BF16)
    y = joined(local) + nn(at_corners, chat[...])
    y_out[...] = y
    pack(y, peers, below, above)
    sums_out[...] = gathered(roll(jnp.where(lane < OWN, 0.0, total), LANES - OWN))


def k_smooth(y, peers, lo, hi, counts, schur_hbm, r_out, m_out, peers_out, below, above, schur, sems):
    rows = [slice(SLAB * i, SLAB * (i + 1)) for i in range(FIELD_PARTS)]
    waits = started([(schur_hbm.at[part, :], schur.at[part, :]) for part in rows], sems)
    r = jump(y, peers, lo, hi, counts, 1.0)
    r_out[...] = r
    r = halves(r)
    m = jnp.zeros((2 * LOADS, LENGTH), F32)
    for part, wait in zip(rows, waits):
        wait.wait()
        m += nn(r[:, part], schur[part, :])
    m = joined(m)
    m_out[...] = m
    pack(m, peers_out, below, above)


def k_search(m, peers, lo, hi, counts, chat, x_out, b_out, msg):
    x = jump(m, peers, lo, hi, counts, 0.25)
    x_out[...] = x
    b = halves(x)
    b_out[...] = b
    terms = joined(nt(b, chat[...])).astype(BF16)
    for g in range(N_GRP):
        msg[g] = terms


def k_search_last(m, peers, lo, hi, counts, chat, r0, p0, q0, x_out, b_out, gram_out, msg):
    w = jump(m, peers, lo, hi, counts, 0.25)
    x_out[...] = w
    b = halves(w)
    b_out[...] = b
    terms = joined(nt(b, chat[...])).astype(BF16)
    for g in range(N_GRP):
        msg[g] = terms
    r, p, q = r0[...], p0[...], q0[...]
    lane = iota((LOADS, LANES), 1)
    gram = jnp.zeros((LOADS, LANES), F32)
    for i, pair in enumerate(((r, p), (p, q), (r, w), (q, w))):
        gram = jnp.where(lane == i, dot_rows(*pair), gram)
    gram_out[...] = gram


def k_finish(
    y, peers, lo, hi, counts, sums, r0, p0, q0, w0, u_hbm, mult_out, res_out, u, sems
):
    rows = [slice(SLAB * i, SLAB * (i + 1)) for i in range(FIELD_PARTS)]
    waits = started([(u_hbm.at[part, :], u.at[part, :]) for part in rows], sems)
    z = jump(y, peers, lo, hi, counts, 1.0)
    rp, pq, rw, qw, local, coarse = (sums[:, i : i + 1] for i in range(6))
    p, q, w = p0[...], q0[...], w0[...]
    first = rp / pq
    inner = rp - first * (rw + pq) + first * first * qw
    grow = 1.0 + inner / rp
    curvature = grow * grow * pq - 2.0 * grow * first * qw + 2.0 * first * first * (local + coarse)
    second = inner / curvature
    mult = first * p + second * (grow * p - first * w)
    res = r0[...] - first * q - second * (grow * q - first * z)
    stacked = jnp.concatenate(list(split3(mult)) + list(split3(res)), axis=0)
    for part, wait in zip(rows, waits):
        wait.wait()
        placed = nt(stacked, u[part, :])
        mult_out[:, part] = placed[0:16] + placed[16:32] + placed[32:48]
        res_out[:, part] = placed[48:64] + placed[64:80] + placed[80:96]


def k_columns(rows, out):
    for g in range(N_GRP):
        out[g] = rows[:, ROWS * g : ROWS * (g + 1)]


def k_permute(u, blocks, out):
    columns = pl.ds(pl.multiple_of(pl.program_id(0) * IFACE, IFACE), IFACE)
    total = jnp.zeros((IFACE, LENGTH), F32)
    for a in range(SUBS):
        rows = slice(IFACE * a, IFACE * (a + 1))
        half = lax.dot_general(
            u[rows, columns], blocks[a], (((0,), (0,)), ((), ())), preferred_element_type=F32
        )
        total += nn(half.astype(BF16), u[rows, :])
    out[...] = total.astype(BF16)


def permuted(u, blocks):
    return pl.pallas_call(
        k_permute,
        grid=(SUBS,),
        out_shape=jax.ShapeDtypeStruct((LENGTH, LENGTH), BF16),
        in_specs=[
            pl.BlockSpec((LENGTH, LENGTH), lambda i: (0, 0)),
            pl.BlockSpec((SUBS, IFACE, IFACE), lambda i: (0, 0, 0)),
        ],
        out_specs=pl.BlockSpec((IFACE, LENGTH), lambda i: (i, 0)),
        compiler_params=pltpu.CompilerParams(vmem_limit_bytes=VMEM_LIMIT),
        name="k_permute",
    )(u, blocks)


FIELD = ((LOADS, LENGTH), F32)
FIELD_B = ((LOADS, LENGTH), BF16)
FIELD_H = ((2 * LOADS, LENGTH), BF16)
OH_LOAD = ((OH_PARTS, ROWS, 4 * LANES), BF16)
OH_PICK = ((PICK_PARTS, COLS, 4 * LANES), BF16)
SQUARE = ((LENGTH, LENGTH), BF16)
PEERS = ((N_SUB, 8, LANES), F32)
SIDE = ((LOADS, SLAB), F32)
TILE = ((LOADS, LANES), F32)
MSG_TERMS = ((N_GRP, LOADS, LANES), BF16)
MSG_LOAD = ((N_SUB, LOADS, ROWS), BF16)
MSG_VALUES = ((N_GRP, LOADS, COLS), BF16)
MSG_CORNERS = ((N_SUB, LOADS, LANES), BF16)


def buffers(kind, parts):
    return (pltpu.VMEM(*kind), pltpu.SemaphoreType.DMA((parts,)))


def over(axis, x):
    return lax.all_to_all(x, axis, split_axis=0, concat_axis=0, tiled=True)


def exchange(peers, below, above):
    up = lax.ppermute(above, "grp", [(i, i + 1) for i in range(N_GRP - 1)])
    down = lax.ppermute(below, "grp", [(i + 1, i) for i in range(N_GRP - 1)])
    return over("sub", peers), up, down


def solve(
    loads,
    boundary_values,
    dirichlet_ids,
    dirichlet_coupling,
    local_inverse,
    local_schur,
    corner_coupling,
    corner_ids,
    coarse_inverse,
    row_counts,
    slot_of,
):
    counts = row_counts[0]
    ids = jnp.pad(corner_ids.reshape(1, OWN), ((0, 0), (0, LANES - OWN)), constant_values=-1)
    where = jnp.stack([lax.axis_index("grp"), lax.axis_index("sub")]).astype(jnp.int32).reshape(1, 2)

    (block,) = call(k_columns, (((N_GRP, CORNERS, ROWS), BF16),), coarse_inverse)
    block = over("grp", block)
    block = block.reshape(COLS, ROWS)

    u, chat, x, msg = call(
        k_setup,
        (
            ((LENGTH, LENGTH), BF16),
            ((LANES, LENGTH), BF16),
            FIELD_B,
            ((N_GRP, LOADS + 8, LANES), BF16),
        ),
        boundary_values,
        dirichlet_ids.reshape(1, SUBS * FIXED),
        dirichlet_coupling[0, 0],
        loads[0, 0],
        slot_of[0],
        corner_coupling[0, 0],
        ids,
        counts,
        smem=(7,),
        hbm=(0, 1, 2, 3, 4, 5),
        out_hbm=(0,),
        scratch=(
            pltpu.VMEM((LOADS, BOUNDARY), F32),
            pltpu.VMEM((1, SUBS * FIXED), jnp.int32),
            pltpu.VMEM((SUBS, IFACE, FIXED), BF16),
            pltpu.VMEM((LOADS, LENGTH), BF16),
            pltpu.VMEM((1, LENGTH), jnp.int32),
            pltpu.VMEM((SUBS, CORNERS, IFACE), BF16),
            pltpu.VMEM((LENGTH, LENGTH), BF16),
            pltpu.SemaphoreType.DMA((6,)),
            pltpu.SemaphoreType.DMA((SUBS,)),
        ),
    )

    inverse = permuted(u, local_inverse[0, 0])
    schur = permuted(u, local_schur[0, 0])

    def local_of(b):
        return jnp.dot(b, inverse, preferred_element_type=F32)

    def smooth(y, got):
        return call(
            k_smooth,
            (FIELD, FIELD, PEERS, SIDE, SIDE),
            y,
            *got,
            counts,
            schur,
            smem=(4,),
            hbm=(5,),
            scratch=buffers(SQUARE, FIELD_PARTS),
        )

    got = over("grp", msg)
    local = local_of(x)
    oh_load, msg = call(
        k_load_first,
        (OH_LOAD, ((N_SUB, LOADS + 8, ROWS), BF16)),
        got,
        ids,
        where,
        smem=(2,),
        out_hbm=(0,),
        scratch=buffers(OH_LOAD, OH_PARTS),
    )
    got = over("sub", msg)
    (oh_pick,) = call(
        k_pick_table,
        (OH_PICK,),
        got,
        where,
        smem=(1,),
        out_hbm=(0,),
        scratch=buffers(OH_PICK, PICK_PARTS),
    )
    (msg,) = call(k_solve, (MSG_VALUES,), got, block)
    got = over("grp", msg)
    (msg,) = call(
        k_pick, (MSG_CORNERS,), got, oh_pick, hbm=(1,), scratch=buffers(OH_PICK, PICK_PARTS)
    )
    got = over("sub", msg)
    y, *parts = call(k_correct, (FIELD, PEERS, SIDE, SIDE), got, chat, local)
    got = exchange(*parts)
    r0, m, *parts = smooth(y, got)
    got = exchange(*parts)

    p0, b, msg = call(k_search, (FIELD, FIELD_H, MSG_TERMS), m, *got, counts, chat, smem=(4,))
    got = over("grp", msg)
    local = local_of(b)
    (msg,) = call(
        k_load, (MSG_LOAD,), got, oh_load, hbm=(1,), scratch=buffers(OH_LOAD, OH_PARTS)
    )
    got = over("sub", msg)
    (msg,) = call(k_solve, (MSG_VALUES,), got, block)
    got = over("grp", msg)
    (msg,) = call(
        k_pick, (MSG_CORNERS,), got, oh_pick, hbm=(1,), scratch=buffers(OH_PICK, PICK_PARTS)
    )
    got = over("sub", msg)
    y, *parts = call(k_correct, (FIELD, PEERS, SIDE, SIDE), got, chat, local)
    got = exchange(*parts)
    q0, m, *parts = smooth(y, got)
    got = exchange(*parts)

    w0, b, gram, msg = call(
        k_search_last,
        (FIELD, FIELD_H, TILE, MSG_TERMS),
        m,
        *got,
        counts,
        chat,
        r0,
        p0,
        q0,
        smem=(4,),
    )
    got = over("grp", msg)
    local = local_of(b)
    (msg,) = call(
        k_load, (MSG_LOAD,), got, oh_load, hbm=(1,), scratch=buffers(OH_LOAD, OH_PARTS)
    )
    got = over("sub", msg)
    wide = ((N_GRP, LOADS, COLS + LANES), BF16)
    (msg,) = call(k_solve_last, (wide,), got, block, gram, w0, local, where, smem=(5,))
    got = over("grp", msg)
    (msg,) = call(
        k_pick_last, (MSG_CORNERS,), got, oh_pick, hbm=(1,), scratch=buffers(OH_PICK, PICK_PARTS)
    )
    got = over("sub", msg)
    y, *parts, sums = call(k_correct_last, (FIELD, PEERS, SIDE, SIDE, TILE), got, chat, local)
    got = exchange(*parts)
    mult, res = call(
        k_finish,
        (FIELD, FIELD),
        y,
        *got,
        counts,
        sums,
        r0,
        p0,
        q0,
        w0,
        u,
        smem=(4,),
        hbm=(10,),
        scratch=buffers(SQUARE, FIELD_PARTS),
    )
    return mult[None, None], res[None, None]


def solution(mesh):
    in_specs = (
        P("grp", "sub", None, None),
        P(),
        P("grp", "sub", None, None),
        P("grp", "sub", None, None, None),
        P("grp", "sub", None, None, None),
        P("grp", "sub", None, None, None),
        P("grp", "sub", None, None, None),
        P("grp", "sub", None, None),
        P(("grp", "sub"), None),
        P("grp", "sub", None),
        P("grp", "sub", None),
    )
    out_specs = (P("grp", "sub", None, None), P("grp", "sub", None, None))
    return jax.shard_map(solve, mesh=mesh, in_specs=in_specs, out_specs=out_specs, check_vma=False)
```

```python
import jax
import jax.numpy as jnp
from jax import lax
from jax.experimental import pallas as pl
from jax.experimental.pallas import tpu as pltpu
from jax.sharding import PartitionSpec as P


IFACE = 512
SUBS = 3
LOADS = 16
CORNERS = 24
FIXED = 128
SLAB = 256
PEER = 64
N_GRP = 32
N_SUB = 16
LENGTH = SUBS * IFACE
WITHIN = N_SUB * PEER
LANES = 128
COARSE = 12288
ROWS = COARSE // N_GRP
COLS = COARSE // N_SUB
OWN = SUBS * CORNERS
BOUNDARY = 6144
F32 = jnp.float32
BF16 = jnp.bfloat16
VMEM_LIMIT = 48 * 1024 * 1024
SELECTS = 4
PICK_PARTS = 4
FIELD_PARTS = 6


def nt(a, b):
    return lax.dot_general(a, b, (((1,), (1,)), ((), ())), preferred_element_type=F32)


def nn(a, b):
    return jnp.dot(a, b, preferred_element_type=F32)


def iota(shape, dim):
    return lax.broadcasted_iota(jnp.int32, shape, dim)


def onehot(test):
    return jnp.where(test, 1.0, 0.0).astype(BF16)


def roll(x, shift):
    return pltpu.roll(x, shift, 1)


def call(body, outs, *args, smem=(), hbm=(), out_hbm=(), scratch=()):
    def place(i, chosen):
        if i in chosen:
            return pl.BlockSpec(memory_space=pltpu.HBM)
        return pl.BlockSpec(memory_space=pltpu.VMEM)

    specs = [
        pl.BlockSpec(memory_space=pltpu.SMEM) if i in smem else place(i, hbm) for i in range(len(args))
    ]
    args = [
        pltpu.with_memory_space_constraint(x, pltpu.HBM) if i in hbm else x for i, x in enumerate(args)
    ]
    return pl.pallas_call(
        body,
        out_shape=[
            pltpu.HBM(s, d) if i in out_hbm else jax.ShapeDtypeStruct(s, d)
            for i, (s, d) in enumerate(outs)
        ],
        in_specs=specs,
        out_specs=[place(i, out_hbm) for i in range(len(outs))],
        scratch_shapes=list(scratch),
        compiler_params=pltpu.CompilerParams(vmem_limit_bytes=VMEM_LIMIT),
    )(*args)


def started(pairs, sems):
    copies = [pltpu.make_async_copy(src, dst, sems.at[i]) for i, (src, dst) in enumerate(pairs)]
    for copy in copies:
        copy.start()
    return copies


def live_mask(counts):
    lane = iota((LOADS, LANES), 1)
    parts = []
    for k in range(N_SUB // 2):
        limit = jnp.where(lane < PEER, counts[0, 2 * k], counts[0, 2 * k + 1] + PEER)
        parts.append(lane < limit)
    for side in range(2):
        for half in range(2):
            parts.append(lane + LANES * half < counts[0, N_SUB + side])
    return [jnp.where(p, 1.0, 0.0) for p in parts]


def pack(y, peers, below, above):
    low = iota((8, LANES), 1) < PEER
    for k in range(N_SUB // 2):
        block = y[:, LANES * k : LANES * (k + 1)]
        top, bottom = block[:8], block[8:]
        peers[2 * k] = jnp.where(low, top, roll(bottom, PEER))
        peers[2 * k + 1] = jnp.where(low, roll(top, PEER), bottom)
    below[...] = y[:, WITHIN : WITHIN + SLAB]
    above[...] = y[:, WITHIN + SLAB :]


def unpack(peers, from_below, from_above):
    low = iota((8, LANES), 1) < PEER
    parts = []
    for k in range(N_SUB // 2):
        m, n = peers[2 * k], peers[2 * k + 1]
        top = jnp.where(low, m, roll(n, PEER))
        bottom = jnp.where(low, roll(m, PEER), n)
        parts.append(jnp.concatenate([top, bottom], axis=0))
    for ref in (from_below, from_above):
        parts += [ref[:, :LANES], ref[:, LANES:]]
    return parts


def jump(y, peers, from_below, from_above, counts, scale):
    masks = live_mask(counts)
    other = unpack(peers, from_below, from_above)
    parts = []
    for k in range(LENGTH // LANES):
        own = y[:, LANES * k : LANES * (k + 1)]
        parts.append(scale * masks[k] * (own - other[k]))
    return jnp.concatenate(parts, axis=1)


def split3(x):
    hi = x.astype(BF16)
    rest = x - hi.astype(F32)
    mid = rest.astype(BF16)
    low = (rest - mid.astype(F32)).astype(BF16)
    return hi, mid, low


def spread(x):
    hi, mid, low = (part.astype(F32) for part in split3(x))
    return hi + roll(mid, 8) + roll(low, 16)


def gathered(x):
    return x + roll(x, LANES - 8) + roll(x, LANES - 16)


def dot_rows(a, b):
    return jnp.sum(a * b, axis=1, keepdims=True)


def k_setup(
    bv_hbm, dids_hbm, dc_hbm, loads_hbm, slots_hbm, corner_hbm, ids, counts,
    u_out, chat_out, x_out, msg,
    bv, dids, dc, loads, slots, corner, u_buf, sems, out_sems,
):
    step = 768
    sources = (slots_hbm, dids_hbm, bv_hbm, corner_hbm, dc_hbm, loads_hbm)
    waits = started(tuple(zip(sources, (slots, dids, bv, corner, dc, loads))), sems)
    waits[0].wait()
    moves = []
    for a in range(SUBS):
        rows = slice(IFACE * a, IFACE * (a + 1))
        u_buf[rows, :] = onehot(iota((IFACE, LENGTH), 0) + IFACE * a == slots[...])
        moves.append(pltpu.make_async_copy(u_buf.at[rows, :], u_out.at[rows, :], out_sems.at[a]))
        moves[-1].start()
    for wait in waits[1:]:
        wait.wait()

    def pick(i, total):
        oh = onehot(iota((step, SUBS * FIXED), 0) + step * i == dids[...])
        part = bv[:, pl.ds(pl.multiple_of(step * i, step), step)]
        return total + nn(part.astype(BF16), oh)

    picked = jnp.zeros((LOADS, SUBS * FIXED), F32)
    picked = lax.fori_loop(0, BOUNDARY // step, pick, picked).astype(BF16)
    x = jnp.zeros((LOADS, LENGTH), F32)
    chat = []
    for a in range(SUBS):
        lifted = nt(picked[:, FIXED * a : FIXED * (a + 1)], dc[a])
        raw = (loads[:, IFACE * a : IFACE * (a + 1)].astype(F32) - lifted).astype(BF16)
        u = u_buf[IFACE * a : IFACE * (a + 1), :]
        x += nn(raw, u)
        chat.append(nn(corner[a], u))
    masks = live_mask(counts)
    x = jnp.concatenate(
        [masks[k] * x[:, LANES * k : LANES * (k + 1)] for k in range(LENGTH // LANES)], axis=1
    ).astype(BF16)
    x_out[...] = x
    chat.append(jnp.zeros((LANES - OWN, LENGTH), F32))
    chat = jnp.concatenate(chat, axis=0).astype(BF16)
    chat_out[...] = chat
    terms = nt(x, chat)
    row = iota((8, LANES), 0)
    high = jnp.broadcast_to(lax.shift_right_arithmetic(ids[...], 7), (8, LANES)).astype(F32)
    low = jnp.broadcast_to(jnp.bitwise_and(ids[...], 127), (8, LANES)).astype(F32)
    table = jnp.where(row == 0, high, jnp.where(row == 1, low, 0.0))
    tile = jnp.concatenate([terms, table], axis=0).astype(BF16)
    for g in range(N_GRP):
        msg[g] = tile
    for move in moves:
        move.wait()


def id_row(tile):
    tile = tile.astype(F32)
    return (tile[0:1] * 128.0 + tile[1:2]).astype(jnp.int32)


def k_load_first(recv, ids, where, msg):
    base = where[0, 0] * ROWS
    load = jnp.zeros((LOADS, ROWS), F32)
    for j in range(N_GRP // 2):
        pair = [recv[2 * j + i] for i in range(2)]
        row = jnp.concatenate([id_row(t[LOADS:]) for t in pair], axis=1)
        oh = onehot(iota((ROWS, 2 * LANES), 0) + base == row)
        load += nt(jnp.concatenate([t[:LOADS] for t in pair], axis=1), oh)
    row = iota((8, LANES), 0)
    high = jnp.broadcast_to(lax.shift_right_arithmetic(ids[...], 7), (8, LANES)).astype(F32)
    low = jnp.broadcast_to(jnp.bitwise_and(ids[...], 127), (8, LANES)).astype(F32)
    table = jnp.where(row == 0, high, jnp.where(row == 1, low, 0.0))
    table = jnp.concatenate([table, jnp.zeros((8, ROWS - LANES), F32)], axis=1)
    tile = jnp.concatenate([load, table], axis=0).astype(BF16)
    for p in range(N_SUB):
        msg[p] = tile


def k_pick_table(recv, where, oh_out, ids_out, oh_buf, sems):
    moves = []
    slab = []
    base = where[0, 1] * CORNERS
    dof = jnp.concatenate(
        [iota((CORNERS, LANES), 0) + (base + ROWS * g) for g in range(N_GRP)], axis=0
    )
    for p in range(N_SUB):
        row = id_row(recv[p, LOADS : LOADS + 8, :LANES])
        slab.append(row[:, :OWN])
        oh_buf[p // 4, :, LANES * (p % 4) : LANES * (p % 4 + 1)] = onehot(dof == row)
        if p % 4 == 3:
            moves.append(pltpu.make_async_copy(oh_buf.at[p // 4], oh_out.at[p // 4], sems.at[p // 4]))
            moves[-1].start()
    ids_out[...] = jnp.concatenate(slab, axis=1)
    for move in moves:
        move.wait()


def slab_load(recv):
    total = recv[0, :LOADS, :].astype(F32)
    for p in range(1, N_SUB):
        total += recv[p, :LOADS, :].astype(F32)
    return total


def halves(x):
    hi = x.astype(BF16)
    return jnp.concatenate([hi, (x - hi.astype(F32)).astype(BF16)], axis=0)


def joined(x):
    if x.shape[0] == LOADS:
        return x[...]
    return x[:LOADS] + x[LOADS:]


def k_solve(recv, block, msg):
    values = joined(nt(halves(slab_load(recv)), block[...])).astype(BF16)
    for g in range(N_GRP):
        msg[g] = values


def coarse_sum(recv, start, size):
    total = recv[0, :, start : start + size].astype(F32)
    for g in range(1, N_GRP):
        total += recv[g, :, start : start + size].astype(F32)
    return total


def pick_starts(oh_hbm, oh, sems):
    return started([(oh_hbm.at[i], oh.at[i]) for i in range(PICK_PARTS)], sems)


def k_pick(recv, oh_hbm, msg, oh, sems):
    waits = pick_starts(oh_hbm, oh, sems)
    values = coarse_sum(recv, 0, COLS).astype(BF16)
    for i, wait in enumerate(waits):
        wait.wait()
        picked = nn(values, oh[i]).astype(BF16)
        for p in range(4):
            msg[4 * i + p] = picked[:, LANES * p : LANES * (p + 1)]


def k_chunk(recv, oh_hbm, msg, oh, sems):
    waits = pick_starts(oh_hbm, oh, sems)
    load = jnp.zeros((LOADS, COLS), F32)
    for i, wait in enumerate(waits):
        terms = jnp.concatenate([recv[4 * i + p] for p in range(4)], axis=1)
        wait.wait()
        load += nt(terms, oh[i])
    load = load.astype(BF16)
    for g in range(N_GRP):
        msg[g] = load


def corner_tiles(recv, rows):
    values = joined(nn(halves(coarse_sum(recv, 0, COLS)), rows[...]))
    pad = jnp.zeros((LOADS, LANES - OWN), F32)
    return [
        jnp.concatenate([values[:, OWN * p : OWN * (p + 1)], pad], axis=1) for p in range(N_SUB)
    ]


def k_corner(recv, rows, msg):
    for p, tile in enumerate(corner_tiles(recv, rows)):
        msg[p] = tile.astype(BF16)


def k_corner_last(recv, rows, terms, gram, field, local, msg):
    tiles = corner_tiles(recv, rows)
    energy = jnp.zeros((LOADS, LANES), F32)
    for p, tile in enumerate(tiles):
        energy += terms[p].astype(F32) * tile
    energy = jnp.sum(energy, axis=1, keepdims=True)
    own = dot_rows(field[...], joined(local))
    lane = iota((LOADS, LANES), 1)
    sums = jnp.where(lane == 4, own, jnp.where(lane == 5, energy, gram[...]))
    sums = roll(spread(sums), OWN)
    for p, tile in enumerate(tiles):
        msg[p] = (tile + sums).astype(BF16)


def corner_sum(recv):
    total = recv[0].astype(F32)
    for p in range(1, N_SUB):
        total += recv[p].astype(F32)
    return total


def k_correct(recv, chat, local, y_out, peers, below, above):
    y = joined(local) + joined(nn(halves(corner_sum(recv)), chat[...]))
    y_out[...] = y
    pack(y, peers, below, above)


def k_correct_last(recv, chat, local, y_out, peers, below, above, sums_out):
    total = corner_sum(recv)
    lane = iota((LOADS, LANES), 1)
    y = joined(local) + joined(nn(halves(jnp.where(lane < OWN, total, 0.0)), chat[...]))
    y_out[...] = y
    pack(y, peers, below, above)
    sums = gathered(roll(jnp.where(lane < OWN, 0.0, total), LANES - OWN))
    tile = spread(jnp.where(lane < 6, sums, 0.0)).astype(BF16)
    for g in range(N_GRP):
        sums_out[g] = tile


def k_smooth(y, peers, lo, hi, counts, schur_hbm, r_out, m_out, peers_out, below, above, schur, sems):
    rows = [slice(SLAB * i, SLAB * (i + 1)) for i in range(FIELD_PARTS)]
    waits = started([(schur_hbm.at[part, :], schur.at[part, :]) for part in rows], sems)
    r = jump(y, peers, lo, hi, counts, 1.0)
    r_out[...] = r
    r = halves(r)
    m = jnp.zeros((2 * LOADS, LENGTH), F32)
    for part, wait in zip(rows, waits):
        wait.wait()
        m += nn(r[:, part], schur[part, :])
    m = joined(m)
    m_out[...] = m
    pack(m, peers_out, below, above)


def k_search(m, peers, lo, hi, counts, chat, x_out, b_out, msg):
    x = jump(m, peers, lo, hi, counts, 0.25)
    x_out[...] = x
    b = halves(x)
    b_out[...] = b
    terms = joined(nt(b, chat[...])).astype(BF16)
    for p in range(N_SUB):
        msg[p] = terms


def k_search_last(m, peers, lo, hi, counts, chat, r0, p0, q0, x_out, b_out, gram_out, msg):
    w = jump(m, peers, lo, hi, counts, 0.25)
    x_out[...] = w
    b = halves(w)
    b_out[...] = b
    terms = joined(nt(b, chat[...])).astype(BF16)
    for p in range(N_SUB):
        msg[p] = terms
    r, p, q = r0[...], p0[...], q0[...]
    lane = iota((LOADS, LANES), 1)
    gram = jnp.zeros((LOADS, LANES), F32)
    for i, pair in enumerate(((r, p), (p, q), (r, w), (q, w))):
        gram = jnp.where(lane == i, dot_rows(*pair), gram)
    gram_out[...] = gram


def k_finish(
    y, peers, lo, hi, counts, sums, r0, p0, q0, w0, u_hbm, mult_out, res_out, u, sems
):
    rows = [slice(SLAB * i, SLAB * (i + 1)) for i in range(FIELD_PARTS)]
    waits = started([(u_hbm.at[part, :], u.at[part, :]) for part in rows], sems)
    z = jump(y, peers, lo, hi, counts, 1.0)
    sums = gathered(coarse_sum(sums, 0, LANES))
    rp, pq, rw, qw, local, coarse = (sums[:, i : i + 1] for i in range(6))
    p, q, w = p0[...], q0[...], w0[...]
    first = rp / pq
    inner = rp - first * (rw + pq) + first * first * qw
    grow = 1.0 + inner / rp
    curvature = grow * grow * pq - 2.0 * grow * first * qw + 2.0 * first * first * (local + coarse)
    second = inner / curvature
    mult = first * p + second * (grow * p - first * w)
    res = r0[...] - first * q - second * (grow * q - first * z)
    stacked = jnp.concatenate([halves(mult), halves(res)], axis=0)
    for part, wait in zip(rows, waits):
        wait.wait()
        placed = nt(stacked, u[part, :])
        mult_out[:, part] = placed[0:16] + placed[16:32]
        res_out[:, part] = placed[32:48] + placed[48:64]


def k_columns(rows, out):
    for g in range(N_GRP):
        out[g] = rows[:, ROWS * g : ROWS * (g + 1)]


def k_permute(u, blocks, out, total):
    columns = pl.ds(pl.multiple_of(pl.program_id(0) * IFACE, IFACE), IFACE)
    total[...] = jnp.zeros_like(total)

    @pl.loop(0, SUBS)
    def _(a):
        rows = pl.ds(pl.multiple_of(a * IFACE, IFACE), IFACE)
        half = lax.dot_general(
            u[rows, columns], blocks[a], (((0,), (0,)), ((), ())), preferred_element_type=F32
        )
        total[...] += nn(half.astype(BF16), u[rows, :])

    out[...] = total[...].astype(BF16)


def permuted(u, blocks):
    return pl.pallas_call(
        k_permute,
        grid=(SUBS,),
        out_shape=jax.ShapeDtypeStruct((LENGTH, LENGTH), BF16),
        in_specs=[
            pl.BlockSpec((LENGTH, LENGTH), lambda i: (0, 0)),
            pl.BlockSpec((SUBS, IFACE, IFACE), lambda i: (0, 0, 0)),
        ],
        out_specs=pl.BlockSpec((IFACE, LENGTH), lambda i: (i, 0)),
        scratch_shapes=[pltpu.VMEM((IFACE, LENGTH), F32)],
        compiler_params=pltpu.CompilerParams(vmem_limit_bytes=VMEM_LIMIT),
        name="k_permute",
    )(u, blocks)


def k_select(first, rows, ids, *refs):
    out, total, oh = refs[-3:]
    i = pl.program_id(0)

    @pl.when(i == 0)
    def _():
        total[...] = refs[0][...].astype(F32) if len(refs) == 4 else jnp.zeros_like(total)

    base = (first[0] + i) * IFACE

    @pl.loop(0, IFACE // LANES)
    def _(j):
        part = pl.ds(pl.multiple_of(j * LANES, LANES), LANES)
        oh[part, :] = onehot(iota((LANES, N_SUB * OWN), 0) + (base + j * LANES) == ids[...])

    @pl.loop(0, COLS // SLAB)
    def _(j):
        part = pl.ds(pl.multiple_of(j * SLAB, SLAB), SLAB)
        total[part, :] += nn(rows[part, :], oh[...])

    @pl.when(i == pl.num_programs(0) - 1)
    def _():
        out[...] = total[...].astype(BF16)


def selected(rows, ids):
    steps = COARSE // IFACE // SELECTS
    shape = (COLS, N_SUB * OWN)
    whole = pl.BlockSpec(shape, lambda i, first: (0, 0))
    table = ()
    for n in range(SELECTS):
        spec = pltpu.PrefetchScalarGridSpec(
            num_scalar_prefetch=1,
            grid=(steps,),
            in_specs=[
                pl.BlockSpec((COLS, IFACE), lambda i, first: (0, first[0] + i)),
                pl.BlockSpec((1, N_SUB * OWN), lambda i, first: (0, 0)),
            ]
            + [whole for _ in table],
            out_specs=whole,
            scratch_shapes=[pltpu.VMEM(shape, F32), pltpu.VMEM((IFACE, shape[1]), BF16)],
        )
        held = [pltpu.with_memory_space_constraint(t, pltpu.HBM) for t in table]
        out = pl.pallas_call(
            k_select,
            grid_spec=spec,
            out_shape=pltpu.HBM(shape, BF16),
            compiler_params=pltpu.CompilerParams(vmem_limit_bytes=VMEM_LIMIT),
            name="k_select",
        )(jnp.full((1,), n * steps, jnp.int32), rows, ids, *held)
        table = (out,)
    return table[0]


FIELD = ((LOADS, LENGTH), F32)
FIELD_B = ((LOADS, LENGTH), BF16)
FIELD_H = ((2 * LOADS, LENGTH), BF16)
OH_PICK = ((PICK_PARTS, COLS, 4 * LANES), BF16)
SQUARE = ((LENGTH, LENGTH), BF16)
PEERS = ((N_SUB, 8, LANES), F32)
SIDE = ((LOADS, SLAB), F32)
TILE = ((LOADS, LANES), F32)
MSG_TERMS = ((N_SUB, LOADS, LANES), BF16)
MSG_VALUES = ((N_GRP, LOADS, COLS), BF16)
MSG_CORNERS = ((N_SUB, LOADS, LANES), BF16)


def buffers(kind, parts):
    return (pltpu.VMEM(*kind), pltpu.SemaphoreType.DMA((parts,)))


def over(axis, x):
    return lax.all_to_all(x, axis, split_axis=0, concat_axis=0, tiled=True)


def exchange(peers, below, above):
    up = lax.ppermute(above, "grp", [(i, i + 1) for i in range(N_GRP - 1)])
    down = lax.ppermute(below, "grp", [(i + 1, i) for i in range(N_GRP - 1)])
    return over("sub", peers), up, down


def solve(
    loads,
    boundary_values,
    dirichlet_ids,
    dirichlet_coupling,
    local_inverse,
    local_schur,
    corner_coupling,
    corner_ids,
    coarse_inverse,
    row_counts,
    slot_of,
):
    counts = row_counts[0]
    ids = jnp.pad(corner_ids.reshape(1, OWN), ((0, 0), (0, LANES - OWN)), constant_values=-1)
    where = jnp.stack([lax.axis_index("grp"), lax.axis_index("sub")]).astype(jnp.int32).reshape(1, 2)

    gathered_rows = lax.all_gather(coarse_inverse, "grp", axis=0, tiled=True)
    (block,) = call(k_columns, (((N_GRP, CORNERS, ROWS), BF16),), coarse_inverse)
    block = over("grp", block).reshape(COLS, ROWS)

    u, chat, x, msg = call(
        k_setup,
        (
            ((LENGTH, LENGTH), BF16),
            ((LANES, LENGTH), BF16),
            FIELD_B,
            ((N_GRP, LOADS + 8, LANES), BF16),
        ),
        boundary_values,
        dirichlet_ids.reshape(1, SUBS * FIXED),
        dirichlet_coupling[0, 0],
        loads[0, 0],
        slot_of[0],
        corner_coupling[0, 0],
        ids,
        counts,
        smem=(7,),
        hbm=(0, 1, 2, 3, 4, 5),
        out_hbm=(0,),
        scratch=(
            pltpu.VMEM((LOADS, BOUNDARY), F32),
            pltpu.VMEM((1, SUBS * FIXED), jnp.int32),
            pltpu.VMEM((SUBS, IFACE, FIXED), BF16),
            pltpu.VMEM((LOADS, LENGTH), BF16),
            pltpu.VMEM((1, LENGTH), jnp.int32),
            pltpu.VMEM((SUBS, CORNERS, IFACE), BF16),
            pltpu.VMEM((LENGTH, LENGTH), BF16),
            pltpu.SemaphoreType.DMA((6,)),
            pltpu.SemaphoreType.DMA((SUBS,)),
        ),
    )

    inverse = permuted(u, local_inverse[0, 0])
    schur = permuted(u, local_schur[0, 0])

    def local_of(b):
        return jnp.dot(b, inverse, preferred_element_type=F32)

    def smooth(y, got):
        return call(
            k_smooth,
            (FIELD, FIELD, PEERS, SIDE, SIDE),
            y,
            *got,
            counts,
            schur,
            smem=(4,),
            hbm=(5,),
            scratch=buffers(SQUARE, FIELD_PARTS),
        )

    got = over("grp", msg)
    local = local_of(x)
    (msg,) = call(
        k_load_first, (((N_SUB, LOADS + 8, ROWS), BF16),), got, ids, where, smem=(2,)
    )
    got = over("sub", msg)
    oh_pick, slab_ids = call(
        k_pick_table,
        (OH_PICK, ((1, N_SUB * OWN), jnp.int32)),
        got,
        where,
        smem=(1,),
        out_hbm=(0,),
        scratch=buffers(OH_PICK, PICK_PARTS),
    )
    (msg,) = call(k_solve, (MSG_VALUES,), got, block)
    got = over("grp", msg)
    (msg,) = call(
        k_pick, (MSG_CORNERS,), got, oh_pick, hbm=(1,), scratch=buffers(OH_PICK, PICK_PARTS)
    )
    got = over("sub", msg)
    y, *parts = call(k_correct, (FIELD, PEERS, SIDE, SIDE), got, chat, local)
    got = exchange(*parts)
    r0, m, *parts = smooth(y, got)
    got = exchange(*parts)
    table = selected(gathered_rows, slab_ids)

    def chunk(got):
        (msg,) = call(
            k_chunk, (MSG_VALUES,), got, oh_pick, hbm=(1,), scratch=buffers(OH_PICK, PICK_PARTS)
        )
        return over("grp", msg)

    p0, b, msg = call(k_search, (FIELD, FIELD_H, MSG_TERMS), m, *got, counts, chat, smem=(4,))
    got = over("sub", msg)
    local = local_of(b)
    got = chunk(got)
    (msg,) = call(k_corner, (MSG_CORNERS,), got, table)
    got = over("sub", msg)
    y, *parts = call(k_correct, (FIELD, PEERS, SIDE, SIDE), got, chat, local)
    got = exchange(*parts)
    q0, m, *parts = smooth(y, got)
    got = exchange(*parts)

    w0, b, gram, msg = call(
        k_search_last,
        (FIELD, FIELD_H, TILE, MSG_TERMS),
        m,
        *got,
        counts,
        chat,
        r0,
        p0,
        q0,
        smem=(4,),
    )
    terms = over("sub", msg)
    local = local_of(b)
    got = chunk(terms)
    (msg,) = call(k_corner_last, (MSG_CORNERS,), got, table, terms, gram, w0, local)
    got = over("sub", msg)
    y, *parts, sums = call(
        k_correct_last,
        (FIELD, PEERS, SIDE, SIDE, ((N_GRP, LOADS, LANES), BF16)),
        got,
        chat,
        local,
    )
    got = exchange(*parts)
    sums = over("grp", sums)
    mult, res = call(
        k_finish,
        (FIELD, FIELD),
        y,
        *got,
        counts,
        sums,
        r0,
        p0,
        q0,
        w0,
        u,
        smem=(4,),
        hbm=(10,),
        scratch=buffers(SQUARE, FIELD_PARTS),
    )
    return mult[None, None], res[None, None]


def solution(mesh):
    in_specs = (
        P("grp", "sub", None, None),
        P(),
        P("grp", "sub", None, None),
        P("grp", "sub", None, None, None),
        P("grp", "sub", None, None, None),
        P("grp", "sub", None, None, None),
        P("grp", "sub", None, None, None),
        P("grp", "sub", None, None),
        P(("grp", "sub"), None),
        P("grp", "sub", None),
        P("grp", "sub", None),
    )
    out_specs = (P("grp", "sub", None, None), P("grp", "sub", None, None))
    return jax.shard_map(solve, mesh=mesh, in_specs=in_specs, out_specs=out_specs, check_vma=False)
```

```python
import jax
import jax.numpy as jnp
from jax import lax
from jax.experimental import pallas as pl
from jax.experimental.pallas import tpu as pltpu
from jax.sharding import PartitionSpec as P


IFACE = 512
SUBS = 3
LOADS = 16
CORNERS = 24
FIXED = 128
SLAB = 256
PEER = 64
N_GRP = 32
N_SUB = 16
LENGTH = SUBS * IFACE
WITHIN = N_SUB * PEER
LANES = 128
COARSE = 12288
ROWS = COARSE // N_GRP
COLS = COARSE // N_SUB
OWN = SUBS * CORNERS
BOUNDARY = 6144
F32 = jnp.float32
BF16 = jnp.bfloat16
VMEM_LIMIT = 48 * 1024 * 1024
LOAD_PARTS = 6
PICK_PARTS = 3
FIELD_PARTS = 6


def nt(a, b):
    return lax.dot_general(a, b, (((1,), (1,)), ((), ())), preferred_element_type=F32)


def nn(a, b):
    return jnp.dot(a, b, preferred_element_type=F32)


def iota(shape, dim):
    return lax.broadcasted_iota(jnp.int32, shape, dim)


def onehot(test):
    return jnp.where(test, 1.0, 0.0).astype(BF16)


def roll(x, shift):
    return pltpu.roll(x, shift, 1)


def call(body, outs, *args, smem=(), hbm=(), out_hbm=(), scratch=()):
    def place(i, chosen):
        if i in chosen:
            return pl.BlockSpec(memory_space=pltpu.HBM)
        return pl.BlockSpec(memory_space=pltpu.VMEM)

    specs = [
        pl.BlockSpec(memory_space=pltpu.SMEM) if i in smem else place(i, hbm) for i in range(len(args))
    ]
    args = [
        pltpu.with_memory_space_constraint(x, pltpu.HBM) if i in hbm else x for i, x in enumerate(args)
    ]
    return pl.pallas_call(
        body,
        out_shape=[
            pltpu.HBM(s, d) if i in out_hbm else jax.ShapeDtypeStruct(s, d)
            for i, (s, d) in enumerate(outs)
        ],
        in_specs=specs,
        out_specs=[place(i, out_hbm) for i in range(len(outs))],
        scratch_shapes=list(scratch),
        compiler_params=pltpu.CompilerParams(vmem_limit_bytes=VMEM_LIMIT),
    )(*args)


def started(pairs, sems):
    copies = [pltpu.make_async_copy(src, dst, sems.at[i]) for i, (src, dst) in enumerate(pairs)]
    for copy in copies:
        copy.start()
    return copies


def live_mask(counts):
    lane = iota((LOADS, LANES), 1)
    parts = []
    for k in range(N_SUB // 2):
        limit = jnp.where(lane < PEER, counts[0, 2 * k], counts[0, 2 * k + 1] + PEER)
        parts.append(lane < limit)
    for side in range(2):
        for half in range(2):
            parts.append(lane + LANES * half < counts[0, N_SUB + side])
    return [jnp.where(p, 1.0, 0.0) for p in parts]


def pack(y, peers, below, above):
    low = iota((8, LANES), 1) < PEER
    for k in range(N_SUB // 2):
        block = y[:, LANES * k : LANES * (k + 1)]
        top, bottom = block[:8], block[8:]
        peers[2 * k] = jnp.where(low, top, roll(bottom, PEER))
        peers[2 * k + 1] = jnp.where(low, roll(top, PEER), bottom)
    below[...] = y[:, WITHIN : WITHIN + SLAB]
    above[...] = y[:, WITHIN + SLAB :]


def unpack(peers, from_below, from_above):
    low = iota((8, LANES), 1) < PEER
    parts = []
    for k in range(N_SUB // 2):
        m, n = peers[2 * k], peers[2 * k + 1]
        top = jnp.where(low, m, roll(n, PEER))
        bottom = jnp.where(low, roll(m, PEER), n)
        parts.append(jnp.concatenate([top, bottom], axis=0))
    for ref in (from_below, from_above):
        parts += [ref[:, :LANES], ref[:, LANES:]]
    return parts


def jump(y, peers, from_below, from_above, counts, scale):
    masks = live_mask(counts)
    other = unpack(peers, from_below, from_above)
    parts = []
    for k in range(LENGTH // LANES):
        own = y[:, LANES * k : LANES * (k + 1)]
        parts.append(scale * masks[k] * (own - other[k]))
    return jnp.concatenate(parts, axis=1)


def split3(x):
    hi = x.astype(BF16)
    rest = x - hi.astype(F32)
    mid = rest.astype(BF16)
    low = (rest - mid.astype(F32)).astype(BF16)
    return hi, mid, low


def spread(x):
    hi, mid, low = (part.astype(F32) for part in split3(x))
    return hi + roll(mid, 8) + roll(low, 16)


def gathered(x):
    return x + roll(x, LANES - 8) + roll(x, LANES - 16)


def dot_rows(a, b):
    return jnp.sum(a * b, axis=1, keepdims=True)


def k_setup(
    bv_hbm, dids_hbm, dc_hbm, loads_hbm, slots_hbm, corner_hbm, inverse_hbm, ids, counts,
    u_out, chat_out, x_out, msg,
    bv, dids, dc, loads, slots, corner, inverse, u_buf, sems, out_sems,
):
    step = 768
    sources = (slots_hbm, dids_hbm, bv_hbm, corner_hbm, dc_hbm, loads_hbm, inverse_hbm)
    waits = started(tuple(zip(sources, (slots, dids, bv, corner, dc, loads, inverse))), sems)
    waits[0].wait()
    moves = []
    for a in range(SUBS):
        rows = slice(IFACE * a, IFACE * (a + 1))
        u_buf[rows, :] = onehot(iota((IFACE, LENGTH), 0) + IFACE * a == slots[...])
        moves.append(pltpu.make_async_copy(u_buf.at[rows, :], u_out.at[rows, :], out_sems.at[a]))
        moves[-1].start()
    for wait in waits[1:]:
        wait.wait()
    picked = jnp.zeros((LOADS, SUBS * FIXED), F32)
    for i in range(BOUNDARY // step):
        oh = onehot(iota((step, SUBS * FIXED), 0) + step * i == dids[...])
        picked += nn(bv[:, step * i : step * (i + 1)].astype(BF16), oh)
    picked = picked.astype(BF16)
    x = jnp.zeros((LOADS, LENGTH), F32)
    chat = []
    for a in range(SUBS):
        lifted = nt(picked[:, FIXED * a : FIXED * (a + 1)], dc[a])
        raw = (loads[:, IFACE * a : IFACE * (a + 1)].astype(F32) - lifted).astype(BF16)
        u = u_buf[IFACE * a : IFACE * (a + 1), :]
        x += nn(raw, u)
        chat.append(nn(corner[a], u))
    masks = live_mask(counts)
    x = jnp.concatenate(
        [masks[k] * x[:, LANES * k : LANES * (k + 1)] for k in range(LENGTH // LANES)], axis=1
    ).astype(BF16)
    x_out[...] = x
    chat.append(jnp.zeros((LANES - OWN, LENGTH), F32))
    chat = jnp.concatenate(chat, axis=0).astype(BF16)
    chat_out[...] = chat
    terms = nt(x, chat)
    row = iota((8, LANES), 0)
    high = jnp.broadcast_to(lax.shift_right_arithmetic(ids[...], 7), (8, LANES)).astype(F32)
    low = jnp.broadcast_to(jnp.bitwise_and(ids[...], 127), (8, LANES)).astype(F32)
    table = jnp.where(row == 0, high, jnp.where(row == 1, low, 0.0))
    tile = jnp.concatenate([terms, table], axis=0).astype(BF16)
    for g in range(N_GRP):
        msg[g, :, :ROWS] = inverse[:, ROWS * g : ROWS * (g + 1)]
        msg[g, :, ROWS:] = tile
    for move in moves:
        move.wait()


def id_row(tile):
    tile = tile.astype(F32)
    return (tile[0:1] * 128.0 + tile[1:2]).astype(jnp.int32)


def k_load_first(recv, ids, where, block_out, msg):
    base = where[0, 0] * ROWS
    load = jnp.zeros((LOADS, ROWS), F32)
    for j in range(N_GRP // 2):
        pair = [recv[2 * j + i, :, ROWS:] for i in range(2)]
        row = jnp.concatenate([id_row(t[LOADS:]) for t in pair], axis=1)
        oh = onehot(iota((ROWS, 2 * LANES), 0) + base == row)
        load += nt(jnp.concatenate([t[:LOADS] for t in pair], axis=1), oh)
    row = iota((8, LANES), 0)
    high = jnp.broadcast_to(lax.shift_right_arithmetic(ids[...], 7), (8, LANES)).astype(F32)
    low = jnp.broadcast_to(jnp.bitwise_and(ids[...], 127), (8, LANES)).astype(F32)
    table = jnp.where(row == 0, high, jnp.where(row == 1, low, 0.0))
    parts = [load[:, LANES * i : LANES * (i + 1)] for i in range(ROWS // LANES)]
    tile = jnp.concatenate(parts + [table], axis=0).astype(BF16)
    for p in range(N_SUB):
        msg[p] = tile
    for g in range(N_GRP):
        block_out[CORNERS * g : CORNERS * (g + 1), :] = recv[g, :, :ROWS]


def write_table(dofs, row, out, buf, sems):
    moves = []
    for i in range(buf.shape[0]):
        buf[i] = onehot(dofs == row[:, ROWS * i : ROWS * (i + 1)])
        moves.append(pltpu.make_async_copy(buf.at[i], out.at[i], sems.at[i]))
        moves[-1].start()
    for move in moves:
        move.wait()


def k_load_table(recv, where, oh_out, oh_buf, sems):
    rows = [id_row(recv[g, LOADS:, ROWS:])[:, :OWN] for g in range(N_GRP)]
    dofs = iota((ROWS, ROWS), 0) + where[0, 0] * ROWS
    write_table(dofs, jnp.concatenate(rows, axis=1), oh_out, oh_buf, sems)


def k_load(recv, oh_hbm, msg, oh, sems):
    waits = started([(oh_hbm.at[i], oh.at[i]) for i in range(LOAD_PARTS)], sems)
    terms = [recv[g].astype(F32)[:, :OWN] for g in range(N_GRP)]
    terms = jnp.concatenate(terms, axis=1).astype(BF16)
    load = jnp.zeros((LOADS, ROWS), F32)
    for i, wait in enumerate(waits):
        wait.wait()
        load += nt(terms[:, ROWS * i : ROWS * (i + 1)], oh[i])
    load = load.astype(BF16)
    for p in range(N_SUB):
        msg[p] = load


def k_pick_table(recv, where, oh_out, oh_buf, sems):
    base = where[0, 1] * CORNERS
    dofs = jnp.concatenate(
        [iota((CORNERS, ROWS), 0) + (base + ROWS * g) for g in range(N_GRP)], axis=0
    )
    rows = [id_row(recv[p, 3 * LOADS :, :])[:, :OWN] for p in range(N_SUB)]
    write_table(dofs, jnp.concatenate(rows, axis=1), oh_out, oh_buf, sems)


def slab_load(recv):
    total = recv[0].astype(F32)
    for p in range(1, N_SUB):
        total += recv[p].astype(F32)
    return total


def halves(x):
    hi = x.astype(BF16)
    return jnp.concatenate([hi, (x - hi.astype(F32)).astype(BF16)], axis=0)


def joined(x):
    if x.shape[0] == LOADS:
        return x[...]
    return x[:LOADS] + x[LOADS:]


def k_solve_first(recv, block, msg):
    total = slab_load(recv)
    load = jnp.concatenate([total[LOADS * i : LOADS * (i + 1)] for i in range(ROWS // LANES)], axis=1)
    values = joined(nt(halves(load), block[...])).astype(BF16)
    for g in range(N_GRP):
        msg[g] = values


def k_solve(recv, block, msg):
    values = joined(nt(halves(slab_load(recv)), block[...])).astype(BF16)
    for g in range(N_GRP):
        msg[g] = values


def k_solve_last(recv, block, gram, field, local, where, msg):
    load = slab_load(recv)
    values = joined(nt(halves(load), block[...])).astype(BF16)
    energy = dot_rows(field[...], joined(local))
    lane = iota((LOADS, LANES), 1)
    sums = roll(spread(jnp.where(lane == 4, energy, gram[...])), CORNERS)
    chunk = jnp.zeros((LOADS, LANES), F32)
    for s in range(N_SUB):
        piece = load[:, CORNERS * s : CORNERS * (s + 1)]
        piece = jnp.concatenate([piece, jnp.zeros((LOADS, LANES - CORNERS), F32)], axis=1)
        chunk = jnp.where(where[0, 1] == s, piece, chunk)
    sums = jnp.where(lane < CORNERS, chunk, sums)
    tile = jnp.concatenate([values, sums.astype(BF16)], axis=1)
    for g in range(N_GRP):
        msg[g] = tile


def coarse_sum(recv, start, size):
    total = recv[0, :, start : start + size].astype(F32)
    for g in range(1, N_GRP):
        total += recv[g, :, start : start + size].astype(F32)
    return total


def corner_tiles(values, waits, oh):
    parts = []
    for i, wait in enumerate(waits):
        wait.wait()
        parts.append(nn(values, oh[i]))
    picked = jnp.concatenate(parts, axis=1)
    pad = jnp.zeros((LOADS, LANES - OWN), F32)
    return [
        jnp.concatenate([picked[:, OWN * p : OWN * (p + 1)], pad], axis=1) for p in range(N_SUB)
    ]


def pick_starts(oh_hbm, oh, sems):
    return started([(oh_hbm.at[i], oh.at[i]) for i in range(PICK_PARTS)], sems)


def k_pick(recv, oh_hbm, msg, oh, sems):
    waits = pick_starts(oh_hbm, oh, sems)
    values = coarse_sum(recv, 0, COLS).astype(BF16)
    for p, tile in enumerate(corner_tiles(values, waits, oh)):
        msg[p] = tile.astype(BF16)


def k_pick_last(recv, oh_hbm, msg, oh, sems):
    waits = pick_starts(oh_hbm, oh, sems)
    values = coarse_sum(recv, 0, COLS)
    lane = iota((LOADS, LANES), 1)
    sums = jnp.where(lane < CORNERS, 0.0, coarse_sum(recv, COLS, LANES))
    sums = gathered(roll(sums, LANES - CORNERS))
    load = [recv[g, :, COLS : COLS + CORNERS].astype(F32) for g in range(N_GRP)]
    energy = dot_rows(jnp.concatenate(load, axis=1), values)
    sums = jnp.where(lane == 5, energy, jnp.where(lane < 5, sums, 0.0))
    sums = roll(spread(sums), OWN)
    for p, tile in enumerate(corner_tiles(values.astype(BF16), waits, oh)):
        msg[p] = (tile + sums).astype(BF16)


def corner_sum(recv):
    total = recv[0].astype(F32)
    for p in range(1, N_SUB):
        total += recv[p].astype(F32)
    return total


def k_correct(recv, chat, local, y_out, peers, below, above):
    y = joined(local) + nn(corner_sum(recv).astype(BF16), chat[...])
    y_out[...] = y
    pack(y, peers, below, above)


def k_correct_last(recv, chat, local, y_out, peers, below, above, sums_out):
    total = corner_sum(recv)
    lane = iota((LOADS, LANES), 1)
    at_corners = jnp.where(lane < OWN, total, 0.0).astype(BF16)
    y = joined(local) + nn(at_corners, chat[...])
    y_out[...] = y
    pack(y, peers, below, above)
    sums_out[...] = gathered(roll(jnp.where(lane < OWN, 0.0, total), LANES - OWN))


def k_smooth(y, peers, lo, hi, counts, schur_hbm, r_out, m_out, peers_out, below, above, schur, sems):
    rows = [slice(SLAB * i, SLAB * (i + 1)) for i in range(FIELD_PARTS)]
    waits = started([(schur_hbm.at[part, :], schur.at[part, :]) for part in rows], sems)
    r = jump(y, peers, lo, hi, counts, 1.0)
    r_out[...] = r
    r = halves(r)
    m = jnp.zeros((2 * LOADS, LENGTH), F32)
    for part, wait in zip(rows, waits):
        wait.wait()
        m += nn(r[:, part], schur[part, :])
    m = joined(m)
    m_out[...] = m
    pack(m, peers_out, below, above)


def k_search(m, peers, lo, hi, counts, chat, x_out, b_out, msg):
    x = jump(m, peers, lo, hi, counts, 0.25)
    x_out[...] = x
    b = halves(x)
    b_out[...] = b
    terms = joined(nt(b, chat[...])).astype(BF16)
    for g in range(N_GRP):
        msg[g] = terms


def k_search_last(m, peers, lo, hi, counts, chat, r0, p0, q0, x_out, b_out, gram_out, msg):
    w = jump(m, peers, lo, hi, counts, 0.25)
    x_out[...] = w
    b = halves(w)
    b_out[...] = b
    terms = joined(nt(b, chat[...])).astype(BF16)
    for g in range(N_GRP):
        msg[g] = terms
    r, p, q = r0[...], p0[...], q0[...]
    lane = iota((LOADS, LANES), 1)
    gram = jnp.zeros((LOADS, LANES), F32)
    for i, pair in enumerate(((r, p), (p, q), (r, w), (q, w))):
        gram = jnp.where(lane == i, dot_rows(*pair), gram)
    gram_out[...] = gram


def k_finish(
    y, peers, lo, hi, counts, sums, r0, p0, q0, w0, u_hbm, mult_out, res_out, u, sems
):
    rows = [slice(SLAB * i, SLAB * (i + 1)) for i in range(FIELD_PARTS)]
    waits = started([(u_hbm.at[part, :], u.at[part, :]) for part in rows], sems)
    z = jump(y, peers, lo, hi, counts, 1.0)
    rp, pq, rw, qw, local, coarse = (sums[:, i : i + 1] for i in range(6))
    p, q, w = p0[...], q0[...], w0[...]
    first = rp / pq
    inner = rp - first * (rw + pq) + first * first * qw
    grow = 1.0 + inner / rp
    curvature = grow * grow * pq - 2.0 * grow * first * qw + 2.0 * first * first * (local + coarse)
    second = inner / curvature
    mult = first * p + second * (grow * p - first * w)
    res = r0[...] - first * q - second * (grow * q - first * z)
    stacked = jnp.concatenate([halves(mult), halves(res)], axis=0)
    for part, wait in zip(rows, waits):
        wait.wait()
        placed = nt(stacked, u[part, :])
        mult_out[:, part] = placed[0:16] + placed[16:32]
        res_out[:, part] = placed[32:48] + placed[48:64]


def k_permute(u, blocks, out):
    columns = pl.ds(pl.multiple_of(pl.program_id(0) * IFACE, IFACE), IFACE)
    total = jnp.zeros((IFACE, LENGTH), F32)
    for a in range(SUBS):
        rows = slice(IFACE * a, IFACE * (a + 1))
        half = lax.dot_general(
            u[rows, columns], blocks[a], (((0,), (0,)), ((), ())), preferred_element_type=F32
        )
        total += nn(half.astype(BF16), u[rows, :])
    out[...] = total.astype(BF16)


def permuted(u, blocks):
    return pl.pallas_call(
        k_permute,
        grid=(SUBS,),
        out_shape=jax.ShapeDtypeStruct((LENGTH, LENGTH), BF16),
        in_specs=[
            pl.BlockSpec((LENGTH, LENGTH), lambda i: (0, 0)),
            pl.BlockSpec((SUBS, IFACE, IFACE), lambda i: (0, 0, 0)),
        ],
        out_specs=pl.BlockSpec((IFACE, LENGTH), lambda i: (i, 0)),
        compiler_params=pltpu.CompilerParams(vmem_limit_bytes=VMEM_LIMIT),
        name="k_permute",
    )(u, blocks)


FIELD = ((LOADS, LENGTH), F32)
FIELD_B = ((LOADS, LENGTH), BF16)
FIELD_H = ((2 * LOADS, LENGTH), BF16)
OH_LOAD = ((LOAD_PARTS, ROWS, ROWS), BF16)
OH_PICK = ((PICK_PARTS, COLS, ROWS), BF16)
SQUARE = ((LENGTH, LENGTH), BF16)
PEERS = ((N_SUB, 8, LANES), F32)
SIDE = ((LOADS, SLAB), F32)
TILE = ((LOADS, LANES), F32)
MSG_TERMS = ((N_GRP, LOADS, LANES), BF16)
MSG_LOAD = ((N_SUB, LOADS, ROWS), BF16)
MSG_VALUES = ((N_GRP, LOADS, COLS), BF16)
MSG_CORNERS = ((N_SUB, LOADS, LANES), BF16)


def buffers(kind, parts):
    return (pltpu.VMEM(*kind), pltpu.SemaphoreType.DMA((parts,)))


def over(axis, x):
    return lax.all_to_all(x, axis, split_axis=0, concat_axis=0, tiled=True)


def exchange(peers, below, above):
    up = lax.ppermute(above, "grp", [(i, i + 1) for i in range(N_GRP - 1)])
    down = lax.ppermute(below, "grp", [(i + 1, i) for i in range(N_GRP - 1)])
    return over("sub", peers), up, down


def solve(
    loads,
    boundary_values,
    dirichlet_ids,
    dirichlet_coupling,
    local_inverse,
    local_schur,
    corner_coupling,
    corner_ids,
    coarse_inverse,
    row_counts,
    slot_of,
):
    counts = row_counts[0]
    ids = jnp.pad(corner_ids.reshape(1, OWN), ((0, 0), (0, LANES - OWN)), constant_values=-1)
    where = jnp.stack([lax.axis_index("grp"), lax.axis_index("sub")]).astype(jnp.int32).reshape(1, 2)

    u, chat, x, msg = call(
        k_setup,
        (
            ((LENGTH, LENGTH), BF16),
            ((LANES, LENGTH), BF16),
            FIELD_B,
            ((N_GRP, CORNERS, ROWS + LANES), BF16),
        ),
        boundary_values,
        dirichlet_ids.reshape(1, SUBS * FIXED),
        dirichlet_coupling[0, 0],
        loads[0, 0],
        slot_of[0],
        corner_coupling[0, 0],
        coarse_inverse,
        ids,
        counts,
        smem=(8,),
        hbm=(0, 1, 2, 3, 4, 5, 6),
        out_hbm=(0,),
        scratch=(
            pltpu.VMEM((LOADS, BOUNDARY), F32),
            pltpu.VMEM((1, SUBS * FIXED), jnp.int32),
            pltpu.VMEM((SUBS, IFACE, FIXED), BF16),
            pltpu.VMEM((LOADS, LENGTH), BF16),
            pltpu.VMEM((1, LENGTH), jnp.int32),
            pltpu.VMEM((SUBS, CORNERS, IFACE), BF16),
            pltpu.VMEM((CORNERS, COARSE), BF16),
            pltpu.VMEM((LENGTH, LENGTH), BF16),
            pltpu.SemaphoreType.DMA((7,)),
            pltpu.SemaphoreType.DMA((SUBS,)),
        ),
    )

    inverse = permuted(u, local_inverse[0, 0])
    schur = permuted(u, local_schur[0, 0])

    def local_of(b):
        return jnp.dot(b, inverse, preferred_element_type=F32)

    def smooth(y, got):
        return call(
            k_smooth,
            (FIELD, FIELD, PEERS, SIDE, SIDE),
            y,
            *got,
            counts,
            schur,
            smem=(4,),
            hbm=(5,),
            scratch=buffers(SQUARE, FIELD_PARTS),
        )

    got = over("grp", msg)
    local = local_of(x)
    block, msg = call(
        k_load_first,
        (((COLS, ROWS), BF16), ((N_SUB, 3 * LOADS + 8, LANES), BF16)),
        got,
        ids,
        where,
        smem=(2,),
    )
    (oh_load,) = call(
        k_load_table,
        (OH_LOAD,),
        got,
        where,
        smem=(1,),
        out_hbm=(0,),
        scratch=buffers(OH_LOAD, LOAD_PARTS),
    )
    got = over("sub", msg)
    (oh_pick,) = call(
        k_pick_table,
        (OH_PICK,),
        got,
        where,
        smem=(1,),
        out_hbm=(0,),
        scratch=buffers(OH_PICK, PICK_PARTS),
    )
    (msg,) = call(k_solve_first, (MSG_VALUES,), got, block)
    got = over("grp", msg)
    (msg,) = call(
        k_pick, (MSG_CORNERS,), got, oh_pick, hbm=(1,), scratch=buffers(OH_PICK, PICK_PARTS)
    )
    got = over("sub", msg)
    y, *parts = call(k_correct, (FIELD, PEERS, SIDE, SIDE), got, chat, local)
    got = exchange(*parts)
    r0, m, *parts = smooth(y, got)
    got = exchange(*parts)

    p0, b, msg = call(k_search, (FIELD, FIELD_H, MSG_TERMS), m, *got, counts, chat, smem=(4,))
    got = over("grp", msg)
    local = local_of(b)
    (msg,) = call(
        k_load, (MSG_LOAD,), got, oh_load, hbm=(1,), scratch=buffers(OH_LOAD, LOAD_PARTS)
    )
    got = over("sub", msg)
    (msg,) = call(k_solve, (MSG_VALUES,), got, block)
    got = over("grp", msg)
    (msg,) = call(
        k_pick, (MSG_CORNERS,), got, oh_pick, hbm=(1,), scratch=buffers(OH_PICK, PICK_PARTS)
    )
    got = over("sub", msg)
    y, *parts = call(k_correct, (FIELD, PEERS, SIDE, SIDE), got, chat, local)
    got = exchange(*parts)
    q0, m, *parts = smooth(y, got)
    got = exchange(*parts)

    w0, b, gram, msg = call(
        k_search_last,
        (FIELD, FIELD_H, TILE, MSG_TERMS),
        m,
        *got,
        counts,
        chat,
        r0,
        p0,
        q0,
        smem=(4,),
    )
    got = over("grp", msg)
    local = local_of(b)
    (msg,) = call(
        k_load, (MSG_LOAD,), got, oh_load, hbm=(1,), scratch=buffers(OH_LOAD, LOAD_PARTS)
    )
    got = over("sub", msg)
    wide = ((N_GRP, LOADS, COLS + LANES), BF16)
    (msg,) = call(k_solve_last, (wide,), got, block, gram, w0, local, where, smem=(5,))
    got = over("grp", msg)
    (msg,) = call(
        k_pick_last, (MSG_CORNERS,), got, oh_pick, hbm=(1,), scratch=buffers(OH_PICK, PICK_PARTS)
    )
    got = over("sub", msg)
    y, *parts, sums = call(k_correct_last, (FIELD, PEERS, SIDE, SIDE, TILE), got, chat, local)
    got = exchange(*parts)
    mult, res = call(
        k_finish,
        (FIELD, FIELD),
        y,
        *got,
        counts,
        sums,
        r0,
        p0,
        q0,
        w0,
        u,
        smem=(4,),
        hbm=(10,),
        scratch=buffers(SQUARE, FIELD_PARTS),
    )
    return mult[None, None], res[None, None]


def solution(mesh):
    in_specs = (
        P("grp", "sub", None, None),
        P(),
        P("grp", "sub", None, None),
        P("grp", "sub", None, None, None),
        P("grp", "sub", None, None, None),
        P("grp", "sub", None, None, None),
        P("grp", "sub", None, None, None),
        P("grp", "sub", None, None),
        P(("grp", "sub"), None),
        P("grp", "sub", None),
        P("grp", "sub", None),
    )
    out_specs = (P("grp", "sub", None, None), P("grp", "sub", None, None))
    return jax.shard_map(solve, mesh=mesh, in_specs=in_specs, out_specs=out_specs, check_vma=False)
```

```python
import jax
import jax.numpy as jnp
from jax import lax
from jax.experimental import pallas as pl
from jax.experimental.pallas import tpu as pltpu
from jax.sharding import PartitionSpec as P


IFACE = 512
SUBS = 3
LOADS = 16
CORNERS = 24
FIXED = 128
SLAB = 256
PEER = 64
N_GRP = 32
N_SUB = 16
LENGTH = SUBS * IFACE
WITHIN = N_SUB * PEER
LANES = 128
COARSE = 12288
ROWS = COARSE // N_GRP
COLS = COARSE // N_SUB
OWN = SUBS * CORNERS
BOUNDARY = 6144
F32 = jnp.float32
BF16 = jnp.bfloat16
VMEM_LIMIT = 48 * 1024 * 1024
LOAD_PARTS = 6
PICK_PARTS = 3
FIELD_PARTS = 6


def nt(a, b):
    return lax.dot_general(a, b, (((1,), (1,)), ((), ())), preferred_element_type=F32)


def nn(a, b):
    return jnp.dot(a, b, preferred_element_type=F32)


def iota(shape, dim):
    return lax.broadcasted_iota(jnp.int32, shape, dim)


def onehot(test):
    return jnp.where(test, 1.0, 0.0).astype(BF16)


def roll(x, shift):
    return pltpu.roll(x, shift, 1)


def call(body, outs, *args, smem=(), hbm=(), out_hbm=(), scratch=()):
    def place(i, chosen):
        if i in chosen:
            return pl.BlockSpec(memory_space=pltpu.HBM)
        return pl.BlockSpec(memory_space=pltpu.VMEM)

    specs = [
        pl.BlockSpec(memory_space=pltpu.SMEM) if i in smem else place(i, hbm) for i in range(len(args))
    ]
    args = [
        pltpu.with_memory_space_constraint(x, pltpu.HBM) if i in hbm else x for i, x in enumerate(args)
    ]
    return pl.pallas_call(
        body,
        out_shape=[
            pltpu.HBM(s, d) if i in out_hbm else jax.ShapeDtypeStruct(s, d)
            for i, (s, d) in enumerate(outs)
        ],
        in_specs=specs,
        out_specs=[place(i, out_hbm) for i in range(len(outs))],
        scratch_shapes=list(scratch),
        compiler_params=pltpu.CompilerParams(vmem_limit_bytes=VMEM_LIMIT),
    )(*args)


def started(pairs, sems):
    copies = [pltpu.make_async_copy(src, dst, sems.at[i]) for i, (src, dst) in enumerate(pairs)]
    for copy in copies:
        copy.start()
    return copies


class Step:
    def __init__(self, copy, later):
        self.copy, self.later = copy, later

    def wait(self):
        self.copy.wait()
        if self.later is not None:
            self.later.start()


def flowing(pairs, sems):
    copies = [pltpu.make_async_copy(src, dst, sems.at[i]) for i, (src, dst) in enumerate(pairs)]
    for copy in copies[:2]:
        copy.start()
    return [Step(copy, later) for copy, later in zip(copies, copies[2:] + [None, None])]


def live_mask(counts):
    lane = iota((LOADS, LANES), 1)
    parts = []
    for k in range(N_SUB // 2):
        limit = jnp.where(lane < PEER, counts[0, 2 * k], counts[0, 2 * k + 1] + PEER)
        parts.append(lane < limit)
    for side in range(2):
        for half in range(2):
            parts.append(lane + LANES * half < counts[0, N_SUB + side])
    return [jnp.where(p, 1.0, 0.0) for p in parts]


def pack(y, peers, below, above):
    low = iota((8, LANES), 1) < PEER
    for k in range(N_SUB // 2):
        block = y[:, LANES * k : LANES * (k + 1)]
        top, bottom = block[:8], block[8:]
        peers[2 * k] = jnp.where(low, top, roll(bottom, PEER))
        peers[2 * k + 1] = jnp.where(low, roll(top, PEER), bottom)
    below[...] = y[:, WITHIN : WITHIN + SLAB]
    above[...] = y[:, WITHIN + SLAB :]


def unpack(peers, from_below, from_above):
    low = iota((8, LANES), 1) < PEER
    parts = []
    for k in range(N_SUB // 2):
        m, n = peers[2 * k], peers[2 * k + 1]
        top = jnp.where(low, m, roll(n, PEER))
        bottom = jnp.where(low, roll(m, PEER), n)
        parts.append(jnp.concatenate([top, bottom], axis=0))
    for ref in (from_below, from_above):
        parts += [ref[:, :LANES], ref[:, LANES:]]
    return parts


def jump(y, peers, from_below, from_above, counts, scale):
    masks = live_mask(counts)
    other = unpack(peers, from_below, from_above)
    parts = []
    for k in range(LENGTH // LANES):
        own = y[:, LANES * k : LANES * (k + 1)]
        parts.append(scale * masks[k] * (own - other[k]))
    return jnp.concatenate(parts, axis=1)


def split3(x):
    hi = x.astype(BF16)
    rest = x - hi.astype(F32)
    mid = rest.astype(BF16)
    low = (rest - mid.astype(F32)).astype(BF16)
    return hi, mid, low


def spread(x):
    hi, mid, low = (part.astype(F32) for part in split3(x))
    return hi + roll(mid, 8) + roll(low, 16)


def gathered(x):
    return x + roll(x, LANES - 8) + roll(x, LANES - 16)


def dot_rows(a, b):
    return jnp.sum(a * b, axis=1, keepdims=True)


def k_setup(
    bv_hbm, dids_hbm, dc_hbm, loads_hbm, slots_hbm, corner_hbm, inverse_hbm, ids, counts,
    u_out, chat_out, x_out, msg,
    bv, dids, dc, loads, slots, corner, inverse, u_buf, sems, out_sems,
):
    step = 768
    sources = (slots_hbm, dids_hbm, bv_hbm, corner_hbm, dc_hbm, loads_hbm, inverse_hbm)
    waits = started(tuple(zip(sources, (slots, dids, bv, corner, dc, loads, inverse))), sems)
    waits[0].wait()
    moves = []
    for a in range(SUBS):
        rows = slice(IFACE * a, IFACE * (a + 1))
        u_buf[rows, :] = onehot(iota((IFACE, LENGTH), 0) + IFACE * a == slots[...])
        moves.append(pltpu.make_async_copy(u_buf.at[rows, :], u_out.at[rows, :], out_sems.at[a]))
        moves[-1].start()
    for wait in waits[1:]:
        wait.wait()
    picked = jnp.zeros((LOADS, SUBS * FIXED), F32)
    for i in range(BOUNDARY // step):
        oh = onehot(iota((step, SUBS * FIXED), 0) + step * i == dids[...])
        picked += nn(bv[:, step * i : step * (i + 1)].astype(BF16), oh)
    picked = picked.astype(BF16)
    x = jnp.zeros((LOADS, LENGTH), F32)
    chat = []
    for a in range(SUBS):
        lifted = nt(picked[:, FIXED * a : FIXED * (a + 1)], dc[a])
        raw = (loads[:, IFACE * a : IFACE * (a + 1)].astype(F32) - lifted).astype(BF16)
        u = u_buf[IFACE * a : IFACE * (a + 1), :]
        x += nn(raw, u)
        chat.append(nn(corner[a], u))
    masks = live_mask(counts)
    x = jnp.concatenate(
        [masks[k] * x[:, LANES * k : LANES * (k + 1)] for k in range(LENGTH // LANES)], axis=1
    ).astype(BF16)
    x_out[...] = x
    chat.append(jnp.zeros((LANES - OWN, LENGTH), F32))
    chat = jnp.concatenate(chat, axis=0).astype(BF16)
    chat_out[...] = chat
    terms = nt(x, chat)
    row = iota((8, LANES), 0)
    high = jnp.broadcast_to(lax.shift_right_arithmetic(ids[...], 7), (8, LANES)).astype(F32)
    low = jnp.broadcast_to(jnp.bitwise_and(ids[...], 127), (8, LANES)).astype(F32)
    table = jnp.where(row == 0, high, jnp.where(row == 1, low, 0.0))
    tile = jnp.concatenate([terms, table], axis=0).astype(BF16)
    for g in range(N_GRP):
        msg[g, :, :ROWS] = inverse[:, ROWS * g : ROWS * (g + 1)]
        msg[g, :, ROWS:] = tile
    for move in moves:
        move.wait()


def id_row(tile):
    tile = tile.astype(F32)
    return (tile[0:1] * 128.0 + tile[1:2]).astype(jnp.int32)


def k_load_first(recv, ids, where, block_out, msg):
    base = where[0, 0] * ROWS
    load = jnp.zeros((LOADS, ROWS), F32)
    for j in range(N_GRP // 2):
        pair = [recv[2 * j + i, :, ROWS:] for i in range(2)]
        row = jnp.concatenate([id_row(t[LOADS:]) for t in pair], axis=1)
        oh = onehot(iota((ROWS, 2 * LANES), 0) + base == row)
        load += nt(jnp.concatenate([t[:LOADS] for t in pair], axis=1), oh)
    row = iota((8, LANES), 0)
    high = jnp.broadcast_to(lax.shift_right_arithmetic(ids[...], 7), (8, LANES)).astype(F32)
    low = jnp.broadcast_to(jnp.bitwise_and(ids[...], 127), (8, LANES)).astype(F32)
    table = jnp.where(row == 0, high, jnp.where(row == 1, low, 0.0))
    parts = [load[:, LANES * i : LANES * (i + 1)] for i in range(ROWS // LANES)]
    tile = jnp.concatenate(parts + [table], axis=0).astype(BF16)
    for p in range(N_SUB):
        msg[p] = tile
    for g in range(N_GRP):
        block_out[CORNERS * g : CORNERS * (g + 1), :] = recv[g, :, :ROWS]


def write_table(dofs, row, out, buf, sems):
    moves = []
    for i in range(buf.shape[0]):
        buf[i] = onehot(dofs == row[:, ROWS * i : ROWS * (i + 1)])
        moves.append(pltpu.make_async_copy(buf.at[i], out.at[i], sems.at[i]))
        moves[-1].start()
    for move in moves:
        move.wait()


def k_load_table(recv, where, oh_out, oh_buf, sems):
    rows = [id_row(recv[g, LOADS:, ROWS:])[:, :OWN] for g in range(N_GRP)]
    dofs = iota((ROWS, ROWS), 0) + where[0, 0] * ROWS
    write_table(dofs, jnp.concatenate(rows, axis=1), oh_out, oh_buf, sems)


def k_load(recv, oh_hbm, msg, oh, sems):
    waits = flowing([(oh_hbm.at[i], oh.at[i]) for i in range(LOAD_PARTS)], sems)
    terms = [recv[g].astype(F32)[:, :OWN] for g in range(N_GRP)]
    terms = jnp.concatenate(terms, axis=1).astype(BF16)
    load = jnp.zeros((LOADS, ROWS), F32)
    for i, wait in enumerate(waits):
        wait.wait()
        load += nt(terms[:, ROWS * i : ROWS * (i + 1)], oh[i])
    load = load.astype(BF16)
    for p in range(N_SUB):
        msg[p] = load


def k_pick_table(recv, where, oh_out, oh_buf, sems):
    base = where[0, 1] * CORNERS
    dofs = jnp.concatenate(
        [iota((CORNERS, ROWS), 0) + (base + ROWS * g) for g in range(N_GRP)], axis=0
    )
    rows = [id_row(recv[p, 3 * LOADS :, :])[:, :OWN] for p in range(N_SUB)]
    write_table(dofs, jnp.concatenate(rows, axis=1), oh_out, oh_buf, sems)


def slab_load(recv):
    total = recv[0].astype(F32)
    for p in range(1, N_SUB):
        total += recv[p].astype(F32)
    return total


def halves(x):
    hi = x.astype(BF16)
    return jnp.concatenate([hi, (x - hi.astype(F32)).astype(BF16)], axis=0)


def joined(x):
    if x.shape[0] == LOADS:
        return x[...]
    return x[:LOADS] + x[LOADS:]


def k_solve_first(recv, block, msg):
    total = slab_load(recv)
    load = jnp.concatenate([total[LOADS * i : LOADS * (i + 1)] for i in range(ROWS // LANES)], axis=1)
    values = joined(nt(halves(load), block[...])).astype(BF16)
    for g in range(N_GRP):
        msg[g] = values


def k_solve(recv, block, msg):
    values = joined(nt(halves(slab_load(recv)), block[...])).astype(BF16)
    for g in range(N_GRP):
        msg[g] = values


def k_solve_last(recv, block, gram, field, local, where, msg):
    load = slab_load(recv)
    values = joined(nt(halves(load), block[...])).astype(BF16)
    energy = dot_rows(field[...], joined(local))
    lane = iota((LOADS, LANES), 1)
    sums = roll(spread(jnp.where(lane == 4, energy, gram[...])), CORNERS)
    chunk = jnp.zeros((LOADS, LANES), F32)
    for s in range(N_SUB):
        piece = load[:, CORNERS * s : CORNERS * (s + 1)]
        piece = jnp.concatenate([piece, jnp.zeros((LOADS, LANES - CORNERS), F32)], axis=1)
        chunk = jnp.where(where[0, 1] == s, piece, chunk)
    sums = jnp.where(lane < CORNERS, chunk, sums)
    tile = jnp.concatenate([values, sums.astype(BF16)], axis=1)
    for g in range(N_GRP):
        msg[g] = tile


def coarse_sum(recv, start, size):
    total = recv[0, :, start : start + size].astype(F32)
    for g in range(1, N_GRP):
        total += recv[g, :, start : start + size].astype(F32)
    return total


def corner_tiles(values, waits, oh):
    parts = []
    for i, wait in enumerate(waits):
        wait.wait()
        parts.append(nn(values, oh[i]))
    picked = jnp.concatenate(parts, axis=1)
    pad = jnp.zeros((LOADS, LANES - OWN), F32)
    return [
        jnp.concatenate([picked[:, OWN * p : OWN * (p + 1)], pad], axis=1) for p in range(N_SUB)
    ]


def pick_starts(oh_hbm, oh, sems):
    return flowing([(oh_hbm.at[i], oh.at[i]) for i in range(PICK_PARTS)], sems)


def k_pick(recv, oh_hbm, msg, oh, sems):
    waits = pick_starts(oh_hbm, oh, sems)
    values = coarse_sum(recv, 0, COLS).astype(BF16)
    for p, tile in enumerate(corner_tiles(values, waits, oh)):
        msg[p] = tile.astype(BF16)


def k_pick_last(recv, oh_hbm, msg, oh, sems):
    waits = pick_starts(oh_hbm, oh, sems)
    values = coarse_sum(recv, 0, COLS)
    lane = iota((LOADS, LANES), 1)
    sums = jnp.where(lane < CORNERS, 0.0, coarse_sum(recv, COLS, LANES))
    sums = gathered(roll(sums, LANES - CORNERS))
    load = [recv[g, :, COLS : COLS + CORNERS].astype(F32) for g in range(N_GRP)]
    energy = dot_rows(jnp.concatenate(load, axis=1), values)
    sums = jnp.where(lane == 5, energy, jnp.where(lane < 5, sums, 0.0))
    sums = roll(spread(sums), OWN)
    for p, tile in enumerate(corner_tiles(values.astype(BF16), waits, oh)):
        msg[p] = (tile + sums).astype(BF16)


def corner_sum(recv):
    total = recv[0].astype(F32)
    for p in range(1, N_SUB):
        total += recv[p].astype(F32)
    return total


def k_correct(recv, chat, local, y_out, peers, below, above):
    y = joined(local) + nn(corner_sum(recv).astype(BF16), chat[...])
    y_out[...] = y
    pack(y, peers, below, above)


def k_correct_last(recv, chat, local, y_out, peers, below, above, sums_out):
    total = corner_sum(recv)
    lane = iota((LOADS, LANES), 1)
    at_corners = jnp.where(lane < OWN, total, 0.0).astype(BF16)
    y = joined(local) + nn(at_corners, chat[...])
    y_out[...] = y
    pack(y, peers, below, above)
    sums_out[...] = gathered(roll(jnp.where(lane < OWN, 0.0, total), LANES - OWN))


def k_smooth(y, peers, lo, hi, counts, schur_hbm, r_out, m_out, peers_out, below, above, schur, sems):
    rows = [slice(SLAB * i, SLAB * (i + 1)) for i in range(FIELD_PARTS)]
    waits = flowing([(schur_hbm.at[part, :], schur.at[part, :]) for part in rows], sems)
    r = jump(y, peers, lo, hi, counts, 1.0)
    r_out[...] = r
    r = halves(r)
    m = jnp.zeros((2 * LOADS, LENGTH), F32)
    for part, wait in zip(rows, waits):
        wait.wait()
        m += nn(r[:, part], schur[part, :])
    m = joined(m)
    m_out[...] = m
    pack(m, peers_out, below, above)


def k_search(m, peers, lo, hi, counts, chat, x_out, b_out, msg):
    x = jump(m, peers, lo, hi, counts, 0.25)
    x_out[...] = x
    b = halves(x)
    b_out[...] = b
    terms = joined(nt(b, chat[...])).astype(BF16)
    for g in range(N_GRP):
        msg[g] = terms


def k_search_last(m, peers, lo, hi, counts, chat, r0, p0, q0, x_out, b_out, gram_out, msg):
    w = jump(m, peers, lo, hi, counts, 0.25)
    x_out[...] = w
    b = halves(w)
    b_out[...] = b
    terms = joined(nt(b, chat[...])).astype(BF16)
    for g in range(N_GRP):
        msg[g] = terms
    r, p, q = r0[...], p0[...], q0[...]
    lane = iota((LOADS, LANES), 1)
    gram = jnp.zeros((LOADS, LANES), F32)
    for i, pair in enumerate(((r, p), (p, q), (r, w), (q, w))):
        gram = jnp.where(lane == i, dot_rows(*pair), gram)
    gram_out[...] = gram


def k_finish(
    y, peers, lo, hi, counts, sums, r0, p0, q0, w0, u_hbm, mult_out, res_out, u, sems
):
    rows = [slice(SLAB * i, SLAB * (i + 1)) for i in range(FIELD_PARTS)]
    waits = flowing([(u_hbm.at[part, :], u.at[part, :]) for part in rows], sems)
    z = jump(y, peers, lo, hi, counts, 1.0)
    rp, pq, rw, qw, local, coarse = (sums[:, i : i + 1] for i in range(6))
    p, q, w = p0[...], q0[...], w0[...]
    first = rp / pq
    inner = rp - first * (rw + pq) + first * first * qw
    grow = 1.0 + inner / rp
    curvature = grow * grow * pq - 2.0 * grow * first * qw + 2.0 * first * first * (local + coarse)
    second = inner / curvature
    mult = first * p + second * (grow * p - first * w)
    res = r0[...] - first * q - second * (grow * q - first * z)
    stacked = jnp.concatenate([halves(mult), halves(res)], axis=0)
    for part, wait in zip(rows, waits):
        wait.wait()
        placed = nt(stacked, u[part, :])
        mult_out[:, part] = placed[0:16] + placed[16:32]
        res_out[:, part] = placed[32:48] + placed[48:64]


def k_permute(u, blocks, out):
    columns = pl.ds(pl.multiple_of(pl.program_id(0) * IFACE, IFACE), IFACE)
    total = jnp.zeros((IFACE, LENGTH), F32)
    for a in range(SUBS):
        rows = slice(IFACE * a, IFACE * (a + 1))
        half = lax.dot_general(
            u[rows, columns], blocks[a], (((0,), (0,)), ((), ())), preferred_element_type=F32
        )
        total += nn(half.astype(BF16), u[rows, :])
    out[...] = total.astype(BF16)


def permuted(u, blocks):
    return pl.pallas_call(
        k_permute,
        grid=(SUBS,),
        out_shape=jax.ShapeDtypeStruct((LENGTH, LENGTH), BF16),
        in_specs=[
            pl.BlockSpec((LENGTH, LENGTH), lambda i: (0, 0)),
            pl.BlockSpec((SUBS, IFACE, IFACE), lambda i: (0, 0, 0)),
        ],
        out_specs=pl.BlockSpec((IFACE, LENGTH), lambda i: (i, 0)),
        compiler_params=pltpu.CompilerParams(vmem_limit_bytes=VMEM_LIMIT),
        name="k_permute",
    )(u, blocks)


FIELD = ((LOADS, LENGTH), F32)
FIELD_B = ((LOADS, LENGTH), BF16)
FIELD_H = ((2 * LOADS, LENGTH), BF16)
OH_LOAD = ((LOAD_PARTS, ROWS, ROWS), BF16)
OH_PICK = ((PICK_PARTS, COLS, ROWS), BF16)
SQUARE = ((LENGTH, LENGTH), BF16)
PEERS = ((N_SUB, 8, LANES), F32)
SIDE = ((LOADS, SLAB), F32)
TILE = ((LOADS, LANES), F32)
MSG_TERMS = ((N_GRP, LOADS, LANES), BF16)
MSG_LOAD = ((N_SUB, LOADS, ROWS), BF16)
MSG_VALUES = ((N_GRP, LOADS, COLS), BF16)
MSG_CORNERS = ((N_SUB, LOADS, LANES), BF16)


def buffers(kind, parts):
    return (pltpu.VMEM(*kind), pltpu.SemaphoreType.DMA((parts,)))


def over(axis, x):
    return lax.all_to_all(x, axis, split_axis=0, concat_axis=0, tiled=True)


def exchange(peers, below, above):
    up = lax.ppermute(above, "grp", [(i, i + 1) for i in range(N_GRP - 1)])
    down = lax.ppermute(below, "grp", [(i + 1, i) for i in range(N_GRP - 1)])
    return over("sub", peers), up, down


def solve(
    loads,
    boundary_values,
    dirichlet_ids,
    dirichlet_coupling,
    local_inverse,
    local_schur,
    corner_coupling,
    corner_ids,
    coarse_inverse,
    row_counts,
    slot_of,
):
    counts = row_counts[0]
    ids = jnp.pad(corner_ids.reshape(1, OWN), ((0, 0), (0, LANES - OWN)), constant_values=-1)
    where = jnp.stack([lax.axis_index("grp"), lax.axis_index("sub")]).astype(jnp.int32).reshape(1, 2)

    u, chat, x, msg = call(
        k_setup,
        (
            ((LENGTH, LENGTH), BF16),
            ((LANES, LENGTH), BF16),
            FIELD_B,
            ((N_GRP, CORNERS, ROWS + LANES), BF16),
        ),
        boundary_values,
        dirichlet_ids.reshape(1, SUBS * FIXED),
        dirichlet_coupling[0, 0],
        loads[0, 0],
        slot_of[0],
        corner_coupling[0, 0],
        coarse_inverse,
        ids,
        counts,
        smem=(8,),
        hbm=(0, 1, 2, 3, 4, 5, 6),
        out_hbm=(0,),
        scratch=(
            pltpu.VMEM((LOADS, BOUNDARY), F32),
            pltpu.VMEM((1, SUBS * FIXED), jnp.int32),
            pltpu.VMEM((SUBS, IFACE, FIXED), BF16),
            pltpu.VMEM((LOADS, LENGTH), BF16),
            pltpu.VMEM((1, LENGTH), jnp.int32),
            pltpu.VMEM((SUBS, CORNERS, IFACE), BF16),
            pltpu.VMEM((CORNERS, COARSE), BF16),
            pltpu.VMEM((LENGTH, LENGTH), BF16),
            pltpu.SemaphoreType.DMA((7,)),
            pltpu.SemaphoreType.DMA((SUBS,)),
        ),
    )

    inverse = permuted(u, local_inverse[0, 0])
    schur = permuted(u, local_schur[0, 0])

    def local_of(b):
        return jnp.dot(b, inverse, preferred_element_type=F32)

    def smooth(y, got):
        return call(
            k_smooth,
            (FIELD, FIELD, PEERS, SIDE, SIDE),
            y,
            *got,
            counts,
            schur,
            smem=(4,),
            hbm=(5,),
            scratch=buffers(SQUARE, FIELD_PARTS),
        )

    got = over("grp", msg)
    local = local_of(x)
    block, msg = call(
        k_load_first,
        (((COLS, ROWS), BF16), ((N_SUB, 3 * LOADS + 8, LANES), BF16)),
        got,
        ids,
        where,
        smem=(2,),
    )
    (oh_load,) = call(
        k_load_table,
        (OH_LOAD,),
        got,
        where,
        smem=(1,),
        out_hbm=(0,),
        scratch=buffers(OH_LOAD, LOAD_PARTS),
    )
    got = over("sub", msg)
    (oh_pick,) = call(
        k_pick_table,
        (OH_PICK,),
        got,
        where,
        smem=(1,),
        out_hbm=(0,),
        scratch=buffers(OH_PICK, PICK_PARTS),
    )
    (msg,) = call(k_solve_first, (MSG_VALUES,), got, block)
    got = over("grp", msg)
    (msg,) = call(
        k_pick, (MSG_CORNERS,), got, oh_pick, hbm=(1,), scratch=buffers(OH_PICK, PICK_PARTS)
    )
    got = over("sub", msg)
    y, *parts = call(k_correct, (FIELD, PEERS, SIDE, SIDE), got, chat, local)
    got = exchange(*parts)
    r0, m, *parts = smooth(y, got)
    got = exchange(*parts)

    p0, b, msg = call(k_search, (FIELD, FIELD_H, MSG_TERMS), m, *got, counts, chat, smem=(4,))
    got = over("grp", msg)
    local = local_of(b)
    (msg,) = call(
        k_load, (MSG_LOAD,), got, oh_load, hbm=(1,), scratch=buffers(OH_LOAD, LOAD_PARTS)
    )
    got = over("sub", msg)
    (msg,) = call(k_solve, (MSG_VALUES,), got, block)
    got = over("grp", msg)
    (msg,) = call(
        k_pick, (MSG_CORNERS,), got, oh_pick, hbm=(1,), scratch=buffers(OH_PICK, PICK_PARTS)
    )
    got = over("sub", msg)
    y, *parts = call(k_correct, (FIELD, PEERS, SIDE, SIDE), got, chat, local)
    got = exchange(*parts)
    q0, m, *parts = smooth(y, got)
    got = exchange(*parts)

    w0, b, gram, msg = call(
        k_search_last,
        (FIELD, FIELD_H, TILE, MSG_TERMS),
        m,
        *got,
        counts,
        chat,
        r0,
        p0,
        q0,
        smem=(4,),
    )
    got = over("grp", msg)
    local = local_of(b)
    (msg,) = call(
        k_load, (MSG_LOAD,), got, oh_load, hbm=(1,), scratch=buffers(OH_LOAD, LOAD_PARTS)
    )
    got = over("sub", msg)
    wide = ((N_GRP, LOADS, COLS + LANES), BF16)
    (msg,) = call(k_solve_last, (wide,), got, block, gram, w0, local, where, smem=(5,))
    got = over("grp", msg)
    (msg,) = call(
        k_pick_last, (MSG_CORNERS,), got, oh_pick, hbm=(1,), scratch=buffers(OH_PICK, PICK_PARTS)
    )
    got = over("sub", msg)
    y, *parts, sums = call(k_correct_last, (FIELD, PEERS, SIDE, SIDE, TILE), got, chat, local)
    got = exchange(*parts)
    mult, res = call(
        k_finish,
        (FIELD, FIELD),
        y,
        *got,
        counts,
        sums,
        r0,
        p0,
        q0,
        w0,
        u,
        smem=(4,),
        hbm=(10,),
        scratch=buffers(SQUARE, FIELD_PARTS),
    )
    return mult[None, None], res[None, None]


def solution(mesh):
    in_specs = (
        P("grp", "sub", None, None),
        P(),
        P("grp", "sub", None, None),
        P("grp", "sub", None, None, None),
        P("grp", "sub", None, None, None),
        P("grp", "sub", None, None, None),
        P("grp", "sub", None, None, None),
        P("grp", "sub", None, None),
        P(("grp", "sub"), None),
        P("grp", "sub", None),
        P("grp", "sub", None),
    )
    out_specs = (P("grp", "sub", None, None), P("grp", "sub", None, None))
    return jax.shard_map(solve, mesh=mesh, in_specs=in_specs, out_specs=out_specs, check_vma=False)
```
